32 devices in a mesh: dp: 2 (over y), wide: 16 (over z, x, core).
Axes of the slice: x: 2, y: 2, z: 4, core: 2. Of those that a mesh axis runs over, the one named last changes fastest.
Arguments:
- patches: bfloat16 [128, 576, 1024], P(('dp', 'wide')), may hold values from -6 to 6
- counts: int32 [32], P(('dp', 'wide')), may hold values from 0 to 4, as said below
- cotangent: bfloat16 [128, 144, 4096], P('dp', None, 'wide'), may hold values from -6 to 6
- filters: float32 [4, 1024, 1024], P(None, ('dp', 'wide')), may hold values from -0.1875 to 0.1875
- filters_moment: float32 [4, 1024, 1024], P(None, ('dp', 'wide')), may hold values from -128 to 128
- filters_square: float32 [4, 1024, 1024], P(None, ('dp', 'wide')), may hold values from 576 to 2304
- filters_average: float32 [4, 1024, 1024], P(None, ('dp', 'wide')), may hold values from -0.1875 to 0.1875
- vectors: float32 [2, 15, 1024], P(None, None, ('dp', 'wide')), as said below
- vectors_moment: float32 [2, 15, 1024], P(None, None, ('dp', 'wide')), may hold values from -256 to 256
- vectors_square: float32 [2, 15, 1024], P(None, None, ('dp', 'wide')), may hold values from 2304 to 9216
- vectors_average: float32 [2, 15, 1024], P(None, None, ('dp', 'wide')), as said below
- expand: float32 [1024, 4096], P(None, 'wide'), may hold values from -0.1875 to 0.1875
- expand_moment: float32 [1024, 4096], P(None, 'wide'), may hold values from -192 to 192
- expand_square: float32 [1024, 4096], P(None, 'wide'), may hold values from 972.8 to 3840
- expand_average: float32 [1024, 4096], P(None, 'wide'), may hold values from -0.1875 to 0.1875
- project: float32 [4096, 4096], P(None, 'wide'), may hold values from -0.09375 to 0.09375
- project_moment: float32 [4096, 4096], P(None, 'wide'), may hold values from -256 to 256
- project_square: float32 [4096, 4096], P(None, 'wide'), may hold values from 1664 to 6656
- project_average: float32 [4096, 4096], P(None, 'wide'), may hold values from -0.09375 to 0.09375
- offsets: float32 [2, 4096], P(None, 'wide'), may hold values from -1.75 to 1.75
- offsets_moment: float32 [2, 4096], P(None, 'wide'), may hold values from -640 to 640
- offsets_square: float32 [2, 4096], P(None, 'wide'), may hold values from 5888 to 23552
- offsets_average: float32 [2, 4096], P(None, 'wide'), may hold values from -1.75 to 1.75
Outputs:
- readout: bfloat16 [128, 144, 4096], P('dp', None, 'wide')
- patch_gradient: bfloat16 [128, 576, 1024], P(('dp', 'wide'))
- filters_updated: float32 [4, 1024, 1024], P(None, ('dp', 'wide'))
- filters_momentum: float32 [4, 1024, 1024], P(None, ('dp', 'wide'))
- filters_variance: float32 [4, 1024, 1024], P(None, ('dp', 'wide'))
- filters_smoothed: float32 [4, 1024, 1024], P(None, ('dp', 'wide'))
- filters_bfloat: bfloat16 [4, 1024, 1024], P(None, ('dp', 'wide'))
- vectors_updated: float32 [2, 15, 1024], P(None, None, ('dp', 'wide'))
- vectors_momentum: float32 [2, 15, 1024], P(None, None, ('dp', 'wide'))
- vectors_variance: float32 [2, 15, 1024], P(None, None, ('dp', 'wide'))
- vectors_smoothed: float32 [2, 15, 1024], P(None, None, ('dp', 'wide'))
- vectors_bfloat: bfloat16 [2, 15, 1024], P(None, None, ('dp', 'wide'))
- expand_updated: float32 [1024, 4096], P(None, 'wide')
- expand_momentum: float32 [1024, 4096], P(None, 'wide')
- expand_variance: float32 [1024, 4096], P(None, 'wide')
- expand_smoothed: float32 [1024, 4096], P(None, 'wide')
- expand_bfloat: bfloat16 [1024, 4096], P(None, 'wide')
- project_updated: float32 [4096, 4096], P(None, 'wide')
- project_momentum: float32 [4096, 4096], P(None, 'wide')
- project_variance: float32 [4096, 4096], P(None, 'wide')
- project_smoothed: float32 [4096, 4096], P(None, 'wide')
- project_bfloat: bfloat16 [4096, 4096], P(None, 'wide')
- offsets_updated: float32 [2, 4096], P(None, 'wide')
- offsets_momentum: float32 [2, 4096], P(None, 'wide')
- offsets_variance: float32 [2, 4096], P(None, 'wide')
- offsets_smoothed: float32 [2, 4096], P(None, 'wide')
- offsets_bfloat: bfloat16 [2, 4096], P(None, 'wide')
The draws below stay inside these ranges and needn't reach their ends.
Inputs may be any that keep to these rules, and one draw needn't show every extreme that they name: counts[s] image slots of sample s hold an image, the slots below counts[s]; some sample has 4. `vectors`: rows 9, 11, 13 of each block are norm gains, rows 10, 12, 14 norm shifts. `vectors_average`: laid out as vectors.
All inputs are finite; a program needn't handle non-finite values.
Results may differ from the reference program's by a relative error of at most 0.023.
The reference program's roundings to bfloat16 on the way count: a program that leaves them out, or rounds other values in their place, can miss the bound.
Values may be sent and summed in bfloat16 or wider, within the bound.
No kernel may reach another device: no remote copies, remote signals or barrier semaphores. Data moves between devices by JAX's collectives and lax.ppermute only.
A program may use at most 512 MiB of HBM per device.

```python
import math
import jax
import jax.numpy as jnp
from jax import lax

D = 1024
OUT = 4096
GRID = 24
POOL = 12
SLOTS = 4
SAMP_DEV = 1
STEP = 3
SAMPLES = 32
IMAGES = 128


def draw_counts(key, part):
    base = jax.random.randint(jax.random.fold_in(key, 1), (SAMPLES,), 0, SLOTS + 1)
    spot = jax.random.randint(jax.random.fold_in(key, 2), (), 0, SAMPLES)
    index = jnp.arange(SAMPLES)
    return jnp.where(index == spot, SLOTS, base).astype(jnp.int32)


def vector_table(key):
    taps = jax.random.normal(jax.random.fold_in(key, 11), (2, 9, D)) * 0.35
    gains = 1.0 + jax.random.uniform(jax.random.fold_in(key, 12), (2, 3, D), minval=-0.3, maxval=0.3)
    shifts = jax.random.normal(jax.random.fold_in(key, 13), (2, 3, D)) * 0.3
    pairs = jnp.stack([gains, shifts], axis=2).reshape(2, 6, D)
    return jnp.concatenate([taps, pairs], axis=1).astype(jnp.float32)


def draw_vectors(key, part):
    return vector_table(jax.random.fold_in(key, 101))


def draw_vectors_average(key, part):
    return vector_table(jax.random.fold_in(key, 202))


def block_scale(own_key, shape, shards, least, top_value):
    level, own = 1.0, jax.random.fold_in(own_key, 6)
    for dim, shards_of in shards:
        steps = jnp.exp(jax.random.uniform(jax.random.fold_in(own, dim), (shards_of,), jnp.float32, least / len(shards), top_value / len(shards)))
        level = level * jnp.repeat(steps, shape[dim] // shards_of).reshape([-1 if axis == dim else 1 for axis in range(len(shape))])
    return level


def noise(rng, extent, scale, bound, pieces=(), kind=jnp.bfloat16):
    entries = scale * jax.random.normal(rng, extent, jnp.float32)
    if pieces:
        entries = entries * block_scale(rng, extent, pieces, -0.22, 0.18)
    return jnp.clip(entries, -bound, bound).astype(kind)


def setup_inputs(seed: int = 0) -> dict:
    splits = jax.random.split(jax.random.key(seed), 24)
    patches = noise(splits[0], (IMAGES, GRID * GRID, D), 1.0, 6.0, ((0, 32),))
    counts = draw_counts(jax.random.fold_in(splits[23], 71), 0)
    cotangent = noise(splits[2], (IMAGES, POOL * POOL, OUT), 1.0, 6.0, ((0, 2), (2, 16)))
    filters = noise(splits[3], (4, D, D), D ** -0.5, 0.1875, ((1, 32),), jnp.float32)
    filters_moment = noise(splits[4], (4, D, D), (0.25 * (72 * IMAGES) ** 0.5), 128.0, ((1, 32),), jnp.float32)
    filters_square = jnp.clip(jnp.exp(math.log(2304.0) - 1.3862944 * jax.random.uniform(splits[5], (4, D, D), jnp.float32) ** block_scale(splits[5], (4, D, D), ((1, 32),), -0.2, 0.2)), 576.0, 2304.0)
    filters_average = noise(splits[6], (4, D, D), D ** -0.5, 0.1875, ((1, 32),), jnp.float32)
    vectors = draw_vectors(jax.random.fold_in(splits[23], 71), 0)
    vectors_moment = noise(splits[8], (2, 15, D), (0.5 * (72 * IMAGES) ** 0.5), 256.0, ((2, 32),), jnp.float32)
    vectors_square = jnp.clip(jnp.exp(math.log(9216.0) - 1.3862944 * jax.random.uniform(splits[9], (2, 15, D), jnp.float32) ** block_scale(splits[9], (2, 15, D), ((2, 32),), -0.2, 0.2)), 2304.0, 9216.0)
    vectors_average = draw_vectors_average(jax.random.fold_in(splits[23], 71), 0)
    expand = noise(splits[11], (D, OUT), D ** -0.5, 0.1875, ((1, 16),), jnp.float32)
    expand_moment = noise(splits[12], (D, OUT), (0.23 * (144 * IMAGES) ** 0.5), 192.0, ((1, 16),), jnp.float32)
    expand_square = jnp.clip(jnp.exp(math.log(3840.0) - 1.3730491 * jax.random.uniform(splits[13], (D, OUT), jnp.float32) ** block_scale(splits[13], (D, OUT), ((1, 16),), -0.2, 0.2)), 972.8, 3840.0)
    expand_average = noise(splits[14], (D, OUT), D ** -0.5, 0.1875, ((1, 16),), jnp.float32)
    project = noise(splits[15], (OUT, OUT), OUT ** -0.5, 0.09375, ((1, 16),), jnp.float32)
    project_moment = noise(splits[16], (OUT, OUT), (0.3 * (144 * IMAGES) ** 0.5), 256.0, ((1, 16),), jnp.float32)
    project_square = jnp.clip(jnp.exp(math.log(6656.0) - 1.3862944 * jax.random.uniform(splits[17], (OUT, OUT), jnp.float32) ** block_scale(splits[17], (OUT, OUT), ((1, 16),), -0.2, 0.2)), 1664.0, 6656.0)
    project_average = noise(splits[18], (OUT, OUT), OUT ** -0.5, 0.09375, ((1, 16),), jnp.float32)
    offsets = noise(splits[19], (2, OUT), 0.3, 1.75, ((1, 16),), jnp.float32)
    offsets_moment = noise(splits[20], (2, OUT), (0.8 * (144 * IMAGES) ** 0.5), 640.0, ((1, 16),), jnp.float32)
    offsets_square = jnp.clip(jnp.exp(math.log(23552.0) - 1.3862944 * jax.random.uniform(splits[21], (2, OUT), jnp.float32) ** block_scale(splits[21], (2, OUT), ((1, 16),), -0.2, 0.2)), 5888.0, 23552.0)
    offsets_average = noise(splits[22], (2, OUT), 0.3, 1.75, ((1, 16),), jnp.float32)
    return {"patches": patches, "counts": counts, "cotangent": cotangent, "filters": filters, "filters_moment": filters_moment, "filters_square": filters_square, "filters_average": filters_average, "vectors": vectors, "vectors_moment": vectors_moment, "vectors_square": vectors_square, "vectors_average": vectors_average, "expand": expand, "expand_moment": expand_moment, "expand_square": expand_square, "expand_average": expand_average, "project": project, "project_moment": project_moment, "project_square": project_square, "project_average": project_average, "offsets": offsets, "offsets_moment": offsets_moment, "offsets_square": offsets_square, "offsets_average": offsets_average}


@jax.custom_vjp
def low(v):
    return lax.optimization_barrier(v.astype(jnp.bfloat16)).astype(jnp.float32)

@jax.custom_vjp
def low_back(v):
    return v

def low_keep(v):
    return (low(v), None)

def low_pass(kept, grad):
    return (grad,)

def back_keep(v):
    return (v, None)

def back_low(kept, grad):
    return (low(grad),)
low.defvjp(low_keep, low_pass)
low_back.defvjp(back_keep, back_low)
beta_one = 0.5
beta_two = 0.5
adam_eps = 1e-08
ema_keep = 0.75
norm_eps = 1e-06

def matmul(left, right):
    return jnp.dot(left, right, preferred_element_type=jnp.float32, precision=lax.Precision.HIGHEST)

def layer_norm(value, gain, shift):
    center = lax.optimization_barrier(jnp.mean(value, axis=-1, keepdims=True))
    centered = value - center
    spread = lax.optimization_barrier(jnp.mean(centered * centered, axis=-1, keepdims=True))
    return centered * lax.rsqrt(spread + norm_eps) * gain + shift

def depthwise(field, taps):
    side = field.shape[1]
    padded = jnp.pad(field, ((0, 0), (1, 1), (1, 1), (0, 0)))
    total = jnp.zeros(field.shape, jnp.float32)
    for row in range(3):
        for column in range(3):
            total = total + padded[:, row:row + side, column:column + side, :] * taps[row * 3 + column]
    return total

def block(rows, w_in, w_out, vecs, side):
    width = rows.shape[1]
    count = rows.shape[0] // (side * side)
    a_lin = low_back(matmul(rows, w_in))
    active = jax.nn.silu(layer_norm(a_lin, vecs[9], vecs[10]))
    mixed = depthwise(active.reshape(count, side, side, width), vecs[0:9]).reshape(count * side * side, width)
    narrow = low(jax.nn.silu(layer_norm(mixed, vecs[11], vecs[12])))
    c_lin = low_back(matmul(narrow, w_out))
    return jax.nn.silu(rows + layer_norm(c_lin, vecs[13], vecs[14]))

def pool(rows, side):
    width = rows.shape[1]
    half = side // 2
    count = rows.shape[0] // (side * side)
    grid = rows.reshape(count, half, 2, half, 2, width)
    return lax.optimization_barrier(jnp.mean(grid, axis=(2, 4))).reshape(count * half * half, width)

def gelu_exact(value):
    return jax.nn.gelu(value, approximate=False)

def adamw(weight, grad, moment, square, average, rate, decay):
    momentum = beta_one * moment + (1.0 - beta_one) * grad
    variance = beta_two * square + (1.0 - beta_two) * grad * grad
    scaled_m = momentum / (1.0 - beta_one ** STEP)
    scaled_v = variance / (1.0 - beta_two ** STEP)
    updated = weight - rate * (scaled_m / (jnp.sqrt(scaled_v) + adam_eps) + decay * weight)
    smoothed = ema_keep * average + (1.0 - ema_keep) * updated
    return (updated, momentum, variance, smoothed, updated.astype(jnp.bfloat16))

def reference(patches, counts, cotangent, filters, filters_moment, filters_square, filters_average, vectors, vectors_moment, vectors_square, vectors_average, expand, expand_moment, expand_square, expand_average, project, project_moment, project_square, project_average, offsets, offsets_moment, offsets_square, offsets_average):
    group = SLOTS * SAMP_DEV
    image_index = jnp.arange(IMAGES, dtype=jnp.int32)
    slot = image_index % SLOTS
    sample = image_index // SLOTS
    live = (slot < counts[sample]).astype(jnp.float32)

    def forward(filters_low, vectors_low, expand_low, project_low, offsets_low, patch_rows):
        batches = patch_rows.reshape(IMAGES // group, group * GRID * GRID, D)
        masks = live.reshape(IMAGES // group, group)

        def abstract(pair):
            rows, mask = pair
            first = block(rows, filters_low[0], filters_low[1], vectors_low[0], GRID)
            pooled = low(pool(first, GRID))
            second = block(pooled, filters_low[2], filters_low[3], vectors_low[1], POOL)
            scale = jnp.repeat(mask, POOL * POOL)[:, None]
            return low(second * scale)
        tokens = lax.map(jax.checkpoint(abstract), (batches, masks))
        tokens = tokens.reshape(IMAGES * POOL * POOL, D)
        pre = low_back(matmul(tokens, expand_low) + offsets_low[0])
        hidden = low(gelu_exact(pre))
        return matmul(hidden, project_low) + offsets_low[1]
    primals = (low(filters), low(vectors), low(expand), low(project), low(offsets), patches.astype(jnp.float32))
    result, pullback = jax.vjp(forward, *primals)
    grads = pullback(cotangent.reshape(IMAGES * POOL * POOL, OUT).astype(jnp.float32))
    readout = result.astype(jnp.bfloat16).reshape(IMAGES, POOL * POOL, OUT)
    patch_gradient = grads[5].astype(jnp.bfloat16)
    filters_out = adamw(filters, grads[0], filters_moment, filters_square, filters_average, 0.03, 0.05)
    vectors_out = adamw(vectors, grads[1], vectors_moment, vectors_square, vectors_average, 0.3, 0.0)
    expand_out = adamw(expand, grads[2], expand_moment, expand_square, expand_average, 0.03, 0.05)
    project_out = adamw(project, grads[3], project_moment, project_square, project_average, 0.016, 0.05)
    offsets_out = adamw(offsets, grads[4], offsets_moment, offsets_square, offsets_average, 0.1, 0.0)
    return (readout, patch_gradient, filters_out[0], filters_out[1], filters_out[2], filters_out[3], filters_out[4], vectors_out[0], vectors_out[1], vectors_out[2], vectors_out[3], vectors_out[4], expand_out[0], expand_out[1], expand_out[2], expand_out[3], expand_out[4], project_out[0], project_out[1], project_out[2], project_out[3], project_out[4], offsets_out[0], offsets_out[1], offsets_out[2], offsets_out[3], offsets_out[4])
```

```python
import math
from functools import partial

import jax
import jax.numpy as jnp
from jax import lax
from jax.experimental import pallas as pl
from jax.experimental.pallas import tpu as pltpu
from jax.sharding import Mesh
from jax.sharding import PartitionSpec as P

GRID = 24
POOL = 12
SLOTS = 4
STEP = 3
LINE = 4
WIDE = ("line", "spot")
ALL = ("dp", "line", "spot")


beta_one = 0.5
beta_two = 0.5
adam_eps = 1e-08
ema_keep = 0.75
norm_eps = 1e-06


def contract_rows(left, right):
    return lax.dot_general(
        left, right, (((0,), (0,)), ((), ())), preferred_element_type=jnp.float32
    )


def contract_cols(left, right):
    return lax.dot_general(
        left, right, (((1,), (1,)), ((), ())), preferred_element_type=jnp.float32
    )


CHUNK = 48
LANE = 128


def shape_of(shape, kind):
    return jax.ShapeDtypeStruct(shape, kind)


def sigmoid(value):
    return 0.5 * jnp.tanh(0.5 * value) + 0.5


def fold_rows(value):
    return jnp.sum(value.reshape(value.shape[0] // 8, 8, value.shape[1]), axis=0)


def row_span(k, size):
    return pl.ds(pl.multiple_of(k * size, 16), size)


def lane_span(j):
    return pl.ds(j * LANE, LANE)


def row_total(parts):
    total = parts[0]
    for part in parts[1:]:
        total = total + part
    return jnp.sum(total, axis=1, keepdims=True)


def normalize(read, norm_ref, scale_ref, span, finish):
    width = norm_ref.shape[1]
    spans = [lane_span(j) for j in range(width // LANE)]
    center = row_total([read(lanes) for lanes in spans]) * (1.0 / width)
    spread = row_total([jnp.square(read(lanes) - center) for lanes in spans]) * (1.0 / width)
    scale = lax.rsqrt(spread + norm_eps)
    scale_ref[span, :] = jnp.broadcast_to(scale, (span.size, LANE))
    for lanes in spans:
        unit = (read(lanes) - center) * scale
        norm_ref[span, lanes] = unit
        finish(lanes, unit)


def shift_rows(value, amount, mask):
    return pltpu.roll(value, amount % value.shape[0], 0) * mask


def masks_for(side, rows):
    cell = jnp.arange(rows, dtype=jnp.int32)
    x, y = cell % side, (cell // side) % side
    flags = jnp.stack([x > 0, x < side - 1, y > 0, y < side - 1]).astype(jnp.float32)
    return jnp.broadcast_to(flags[:, :, None], (4, rows, LANE))


def conv_block(above, level, below, taps, mask_ref):
    columns = [
        taps[c] * above + taps[3 + c] * level + taps[6 + c] * below for c in range(3)
    ]
    return (
        columns[1]
        + shift_rows(columns[0], 1, mask_ref[0])
        + shift_rows(columns[2], -1, mask_ref[1])
    )


def taps_at(vec_ref, lanes):
    return [vec_ref[k : k + 1, lanes] for k in range(9)]


def forward_kernel(side, *refs):
    pooled = side == GRID
    if pooled:
        x_ref, in_ref, out_ref, vec_ref, mask_ref, pool_ref = refs[:6]
        n1_ref, n2_ref, n3_ref, r1_ref, r2_ref, r3_ref, b_ref, y_ref = refs[6:14]
        lin_ref, act_ref, hi_ref, lo_ref = refs[14:]
    else:
        live_ref, x_ref, in_ref, out_ref, vec_ref, mask_ref = refs[:6]
        n1_ref, n2_ref, n3_ref, r1_ref, r2_ref, r3_ref, b_ref, y_ref = refs[6:14]
        lin_ref, act_ref = refs[14:]
    rows, width = x_ref.shape
    count = rows // CHUNK
    edge = side if pooled else 0
    lin_ref[...] = jnp.dot(x_ref[...], in_ref[...], preferred_element_type=jnp.float32)
    if pooled:
        act_ref[0:side, :] = jnp.zeros((side, width), jnp.float32)
        act_ref[rows + side : rows + 2 * side, :] = jnp.zeros((side, width), jnp.float32)

    @pl.loop(0, count)
    def _(k):
        span = row_span(k, CHUNK)
        above = pl.ds(pl.multiple_of(k * CHUNK + edge, 8), CHUNK)

        def finish(lanes, unit):
            value = unit * vec_ref[9:10, lanes] + vec_ref[10:11, lanes]
            act_ref[above, lanes] = value * sigmoid(value)

        normalize(lambda lanes: lin_ref[span, lanes], n1_ref, r1_ref, span, finish)

    if pooled:

        @pl.loop(0, count)
        def _(k):
            for j in range(width // LANE):
                lanes = lane_span(j)
                near = [
                    act_ref[pl.ds(pl.multiple_of(k * CHUNK + r * side, 8), CHUNK), lanes]
                    for r in range(3)
                ]
                lin_ref[row_span(k, CHUNK), lanes] = conv_block(
                    near[0], near[1], near[2], taps_at(vec_ref, lanes), mask_ref
                )
    else:
        cells = side * side

        @pl.loop(0, rows // cells)
        def _(k):
            for j in range(width // LANE):
                lanes = lane_span(j)
                level = act_ref[row_span(k, cells), lanes]
                lin_ref[row_span(k, cells), lanes] = conv_block(
                    shift_rows(level, side, mask_ref[2]),
                    level,
                    shift_rows(level, -side, mask_ref[3]),
                    taps_at(vec_ref, lanes),
                    mask_ref,
                )

    @pl.loop(0, count)
    def _(k):
        span = row_span(k, CHUNK)

        def finish(lanes, unit):
            value = unit * vec_ref[11:12, lanes] + vec_ref[12:13, lanes]
            b_ref[span, lanes] = (value * sigmoid(value)).astype(jnp.bfloat16)

        normalize(lambda lanes: lin_ref[span, lanes], n2_ref, r2_ref, span, finish)

    lin_ref[...] = jnp.dot(b_ref[...], out_ref[...], preferred_element_type=jnp.float32)

    @pl.loop(0, count)
    def _(k):
        span = row_span(k, CHUNK)
        if not pooled:
            scale = live_ref[k * CHUNK // (side * side)]

        def finish(lanes, unit):
            value = (
                x_ref[span, lanes].astype(jnp.float32)
                + unit * vec_ref[13:14, lanes]
                + vec_ref[14:15, lanes]
            )
            value = value * sigmoid(value)
            if pooled:
                high = value.astype(jnp.bfloat16)
                hi_ref[span, lanes] = high
                lo_ref[span, lanes] = (value - high.astype(jnp.float32)).astype(jnp.bfloat16)
            else:
                y_ref[span, lanes] = (value * scale).astype(jnp.bfloat16)

        normalize(lambda lanes: lin_ref[span, lanes], n3_ref, r3_ref, span, finish)

    if pooled:
        y_ref[...] = (
            jnp.dot(pool_ref[...], hi_ref[...], preferred_element_type=jnp.float32)
            + jnp.dot(pool_ref[...], lo_ref[...], preferred_element_type=jnp.float32)
        ).astype(jnp.bfloat16)


def backward_kernel(side, *refs):
    pooled = side == GRID
    if pooled:
        up_ref, d_ref, x_ref, in_ref, out_ref, vec_ref, mask_ref = refs[:7]
    else:
        live_ref, d_ref, x_ref, in_ref, out_ref, vec_ref, mask_ref = refs[:7]
    n1_ref, n2_ref, n3_ref, r1_ref, r2_ref, r3_ref = refs[7:13]
    dx_ref, da_ref, dc_ref, sum_ref = refs[13:17]
    res_ref, mix_ref, act_ref = refs[17:20]
    rows, width = x_ref.shape
    count = rows // CHUNK
    edge = side if pooled else 0
    spans = [lane_span(j) for j in range(width // LANE)]

    @pl.when(pl.program_id(0) == 0)
    def _():
        sum_ref[...] = jnp.zeros(sum_ref.shape, jnp.float32)

    def add_sum(k, lanes, value):
        sum_ref[8 * k : 8 * k + 8, lanes] += fold_rows(value)

    if pooled:
        grads = d_ref[...]
        high = grads.astype(jnp.bfloat16)
        low = (grads - high.astype(jnp.float32)).astype(jnp.bfloat16)
        res_ref[...] = jnp.dot(
            up_ref[...], high, preferred_element_type=jnp.float32
        ) + jnp.dot(up_ref[...], low, preferred_element_type=jnp.float32)

    def norm_back(unit_ref, scale_ref, span, gain, read_grad, store):
        first, second = [], []
        for lanes in spans:
            grad = read_grad(lanes) * vec_ref[gain : gain + 1, lanes]
            first.append(grad)
            second.append(grad * unit_ref[span, lanes])
        mean_grad = row_total(first) * (1.0 / width)
        mean_unit = row_total(second) * (1.0 / width)
        for lanes in spans:
            grad = read_grad(lanes) * vec_ref[gain : gain + 1, lanes]
            store(
                lanes,
                scale_ref[span, :]
                * (grad - mean_grad - unit_ref[span, lanes] * mean_unit),
            )

    @pl.loop(0, count)
    def _(k):
        span = row_span(k, CHUNK)
        if not pooled:
            scale = live_ref[k * CHUNK // (side * side)]
        for lanes in spans:
            unit = n3_ref[span, lanes]
            value = (
                x_ref[span, lanes].astype(jnp.float32)
                + unit * vec_ref[13:14, lanes]
                + vec_ref[14:15, lanes]
            )
            gate = sigmoid(value)
            grad = res_ref[span, lanes] if pooled else d_ref[span, lanes] * scale
            grad = grad * (gate * (1.0 + value * (1.0 - gate)))
            res_ref[span, lanes] = grad
            add_sum(13, lanes, grad * unit)
            add_sum(14, lanes, grad)

        def store(lanes, value):
            dc_ref[span, lanes] = value.astype(jnp.bfloat16)

        norm_back(n3_ref, r3_ref, span, 13, lambda lanes: res_ref[span, lanes], store)

    if pooled:
        mix_ref[0:side, :] = jnp.zeros((side, width), jnp.float32)
        mix_ref[rows + side : rows + 2 * side, :] = jnp.zeros((side, width), jnp.float32)
    mix_ref[edge : rows + edge, :] = contract_cols(dc_ref[...], out_ref[...])

    @pl.loop(0, count)
    def _(k):
        span = row_span(k, CHUNK)
        at = pl.ds(pl.multiple_of(k * CHUNK + edge, 8), CHUNK)
        for lanes in spans:
            unit = n2_ref[span, lanes]
            value = unit * vec_ref[11:12, lanes] + vec_ref[12:13, lanes]
            gate = sigmoid(value)
            grad = mix_ref[at, lanes] * (gate * (1.0 + value * (1.0 - gate)))
            mix_ref[at, lanes] = grad
            add_sum(11, lanes, grad * unit)
            add_sum(12, lanes, grad)

        def store(lanes, value):
            mix_ref[at, lanes] = value

        norm_back(n2_ref, r2_ref, span, 11, lambda lanes: mix_ref[at, lanes], store)

    size = CHUNK if pooled else side * side

    @pl.loop(0, rows // size)
    def _(k):
        span = row_span(k, size)
        for lanes in spans:
            if pooled:
                near = [
                    mix_ref[pl.ds(pl.multiple_of(k * size + (2 - r) * side, 8), size), lanes]
                    for r in range(3)
                ]
            else:
                level = mix_ref[span, lanes]
                near = [
                    shift_rows(level, -side, mask_ref[3]),
                    level,
                    shift_rows(level, side, mask_ref[2]),
                ]
            taps = taps_at(vec_ref, lanes)
            mixed = [
                taps[c] * near[0] + taps[3 + c] * near[1] + taps[6 + c] * near[2]
                for c in range(3)
            ]
            grad = (
                mixed[1]
                + shift_rows(mixed[0], -1, mask_ref[1])
                + shift_rows(mixed[2], 1, mask_ref[0])
            )
            unit = n1_ref[span, lanes]
            value = unit * vec_ref[9:10, lanes] + vec_ref[10:11, lanes]
            gate = sigmoid(value)
            active = value * gate
            sides = [
                shift_rows(active, 1, mask_ref[0]),
                active,
                shift_rows(active, -1, mask_ref[1]),
            ]
            for r in range(3):
                for c in range(3):
                    add_sum(3 * r + c, lanes, sides[c] * near[r])
            grad = grad * (gate * (1.0 + value * (1.0 - gate)))
            act_ref[span, lanes] = grad
            add_sum(9, lanes, grad * unit)
            add_sum(10, lanes, grad)

    @pl.loop(0, count)
    def _(k):
        span = row_span(k, CHUNK)

        def store(lanes, value):
            da_ref[span, lanes] = value.astype(jnp.bfloat16)

        norm_back(n1_ref, r1_ref, span, 9, lambda lanes: act_ref[span, lanes], store)

    step = 256
    for j in range(width // step):
        dx_ref[:, j * step : (j + 1) * step] = (
            res_ref[:, j * step : (j + 1) * step]
            + contract_cols(da_ref[...], in_ref[j * step : (j + 1) * step, :])
        ).astype(dx_ref.dtype)


def pool_matrix():
    cell = jnp.arange(GRID * GRID, dtype=jnp.int32)
    home = (cell // GRID // 2) * POOL + (cell % GRID) // 2
    spot = jnp.arange(POOL * POOL, dtype=jnp.int32)
    return jnp.where(home[None, :] == spot[:, None], 0.25, 0.0).astype(jnp.bfloat16)


def block_specs(side, rows, width):
    whole = lambda shape: pl.BlockSpec(shape, lambda i: (0,) * len(shape))
    part = lambda cells, lanes: pl.BlockSpec((cells, lanes), lambda i: (i, 0))
    size = side * side if side == GRID else rows
    return whole, part, size


def kernel_params(axes=1):
    return pltpu.CompilerParams(
        dimension_semantics=("arbitrary",) * axes, vmem_limit_bytes=60 * 1024 * 1024
    )


def block_forward(rows, w_in, w_out, vecs, side, live=None):
    total, width = rows.shape
    whole, part, size = block_specs(side, total, width)
    pooled = side == GRID
    mask_rows = CHUNK if pooled else side * side
    vecs = jnp.pad(vecs, ((0, 1), (0, 0)))
    masks = masks_for(side, mask_rows)
    norm = shape_of((total, width), jnp.float32)
    scale = shape_of((total, LANE), jnp.float32)
    out_cells = POOL * POOL if pooled else size
    operands = [rows, w_in, w_out, vecs, masks]
    in_specs = [
        part(size, width),
        whole(w_in.shape),
        whole(w_out.shape),
        whole(vecs.shape),
        whole(masks.shape),
    ]
    scratch = [
        pltpu.VMEM((size, width), jnp.float32),
        pltpu.VMEM((size + 2 * side, width) if pooled else (size, width), jnp.float32),
    ]
    if pooled:
        operands.append(pool_matrix())
        in_specs.append(whole((POOL * POOL, GRID * GRID)))
        scratch += [pltpu.VMEM((size, width), jnp.bfloat16)] * 2
    else:
        operands.insert(0, live)
        in_specs.insert(0, pl.BlockSpec(memory_space=pltpu.SMEM))
    outs = pl.pallas_call(
        partial(forward_kernel, side),
        grid=(total // size,),
        in_specs=in_specs,
        out_specs=[part(size, width)] * 3
        + [part(size, LANE)] * 3
        + [part(size, width), part(out_cells, width)],
        out_shape=[norm] * 3
        + [scale] * 3
        + [
            shape_of((total, width), jnp.bfloat16),
            shape_of((total // size * out_cells, width), jnp.bfloat16),
        ],
        scratch_shapes=scratch,
        compiler_params=kernel_params(),
        name="block_forward_" + str(side),
    )(*operands)
    return outs[7], (rows, outs[6], tuple(outs[:6]))


def block_backward(d_result, saved, w_in, w_out, vecs, side, live=None):
    rows, narrow, kept = saved
    total, width = rows.shape
    whole, part, size = block_specs(side, total, width)
    pooled = side == GRID
    mask_rows = CHUNK if pooled else side * side
    vecs = jnp.pad(vecs, ((0, 1), (0, 0)))
    masks = masks_for(side, mask_rows)
    in_cells = POOL * POOL if pooled else size
    if pooled:
        first = pool_matrix().T
        first_spec = whole(first.shape)
    else:
        first = live
        first_spec = pl.BlockSpec(memory_space=pltpu.SMEM)
    low = shape_of((total, width), jnp.bfloat16)
    dx, da, dc, sums = pl.pallas_call(
        partial(backward_kernel, side),
        grid=(total // size,),
        in_specs=[
            first_spec,
            part(in_cells, width),
            part(size, width),
            whole(w_in.shape),
            whole(w_out.shape),
            whole(vecs.shape),
            whole(masks.shape),
        ]
        + [part(size, width)] * 3
        + [part(size, LANE)] * 3,
        out_specs=[part(size, width)] * 3 + [whole((128, width))],
        out_shape=[
            shape_of((total, width), jnp.bfloat16 if pooled else jnp.float32),
            low,
            low,
            shape_of((128, width), jnp.float32),
        ],
        scratch_shapes=[
            pltpu.VMEM((size, width), jnp.float32),
            pltpu.VMEM((size + 2 * side, width) if pooled else (size, width), jnp.float32),
            pltpu.VMEM((size, width), jnp.float32),
        ],
        compiler_params=kernel_params(),
        name="block_backward_" + str(side),
    )(first, d_result, rows, w_in, w_out, vecs, masks, *kept)
    grad_out = contract_rows(narrow, dc)
    grad_in = contract_rows(rows, da)
    grad_vecs = jnp.sum(sums[:120].reshape(15, 8, width), axis=1)
    return dx, grad_in, grad_out, grad_vecs


def adamw(weight, grad, moment, square, average, rate, decay):
    momentum = beta_one * moment + (1.0 - beta_one) * grad
    variance = beta_two * square + (1.0 - beta_two) * grad * grad
    scaled_m = momentum / (1.0 - beta_one**STEP)
    scaled_v = variance / (1.0 - beta_two**STEP)
    updated = weight - rate * (scaled_m / (jnp.sqrt(scaled_v) + adam_eps) + decay * weight)
    smoothed = ema_keep * average + (1.0 - ema_keep) * updated
    return (updated, momentum, variance, smoothed, updated.astype(jnp.bfloat16))


def pad_row(row, width):
    return jnp.pad(row, ((0, 0), (0, width - row.shape[1])))


def over_groups(value, group):
    if group == 2:
        other = lax.ppermute(value, "dp", [(0, 1), (1, 0)])
        return value.astype(jnp.float32) + other.astype(jnp.float32)
    return lax.psum(value, "dp").astype(jnp.float32)


def reduce_block(grad_in, grad_out, grad_vecs, devices):
    width = grad_in.shape[1]
    share = width // devices
    rows = [
        grad_in.astype(jnp.bfloat16).reshape(devices, share, width),
        grad_out.astype(jnp.bfloat16).reshape(devices, share, width),
        jnp.pad(
            grad_vecs.astype(jnp.bfloat16)
            .reshape(15, devices, share)
            .transpose(1, 0, 2)
            .reshape(devices, 1, 15 * share),
            ((0, 0), (0, 15), (0, width - 15 * share)),
        ),
    ]
    return jnp.concatenate(rows, axis=1)


def pick(value, at, axis):
    return lax.dynamic_index_in_dim(value, at, axis, False)


def halve_blocks(blocks, order):
    count = blocks.shape[0]
    bits = count.bit_length() - 1
    me = lax.axis_index(ALL)
    blocks = blocks.reshape((2,) * bits + blocks.shape[1:])
    left = list(range(bits))[::-1]
    for bit in order:
        axis = left.index(bit)
        left.pop(axis)
        mine = (me >> bit) & 1
        pairs = [(i, i ^ (1 << bit)) for i in range(count)]
        theirs = lax.ppermute(pick(blocks, 1 - mine, axis), ALL, pairs)
        blocks = (
            pick(blocks, mine, axis).astype(jnp.float32) + theirs.astype(jnp.float32)
        ).astype(jnp.bfloat16)
    return blocks


def spread_reduce(blocks):
    bits = blocks.shape[0].bit_length() - 1
    return halve_blocks(blocks, [0, 1] + list(range(bits - 1, 1, -1)))


def held(value):
    return lax.optimization_barrier(value)


def gelu_slope(value):
    return 0.5 * (1.0 + lax.erf(value * (0.5**0.5))) + value * jnp.exp(-0.5 * value * value) * (
        0.5 / math.pi
    ) ** 0.5


def hidden_kernel(tokens_ref, expand_ref, bias_ref, out_ref):
    pre = jnp.dot(tokens_ref[...], expand_ref[...], preferred_element_type=jnp.float32)
    pre = pre + bias_ref[...]
    out_ref[...] = (0.5 * pre * (1.0 + lax.erf(pre * (0.5**0.5)))).astype(jnp.bfloat16)


def hidden_forward(tokens, readers, bias):
    total, width = tokens.shape
    depth = readers.shape[1]
    rows, step = total // LINE, 512
    return pl.pallas_call(
        hidden_kernel,
        grid=(depth // step, LINE),
        in_specs=[
            pl.BlockSpec((rows, width), lambda j, i: (i, 0)),
            pl.BlockSpec((width, step), lambda j, i: (0, j)),
            pl.BlockSpec((1, step), lambda j, i: (0, j)),
        ],
        out_specs=pl.BlockSpec((rows, step), lambda j, i: (i, j)),
        out_shape=shape_of((total, depth), jnp.bfloat16),
        compiler_params=kernel_params(2),
        name="hidden_forward",
    )(tokens, readers, bias[None])


def adamw_kernel(rate, decay, grad_ref, *refs):
    old, new = refs[:4], refs[4:]
    results = adamw(old[0][...], grad_ref[...].T, *[ref[...] for ref in old[1:]], rate, decay)
    for ref, result in zip(new, results):
        ref[...] = result


def adamw_turned(weight, grad, moment, square, average, rate, decay):
    depth, columns = weight.shape
    step = 512
    part = pl.BlockSpec((step, columns), lambda i: (i, 0))
    return pl.pallas_call(
        partial(adamw_kernel, rate, decay),
        grid=(depth // step,),
        in_specs=[pl.BlockSpec((columns, step), lambda i: (0, i))] + [part] * 4,
        out_specs=[part] * 5,
        out_shape=[shape_of(weight.shape, jnp.float32)] * 4
        + [shape_of(weight.shape, jnp.bfloat16)],
        compiler_params=kernel_params(),
        name="adamw_turned",
    )(grad, weight, moment, square, average)


def pre_kernel(d_ref, tokens_ref, project_ref, expand_ref, bias_ref, out_ref):
    grad = contract_cols(d_ref[...], project_ref[...])
    pre = jnp.dot(tokens_ref[...], expand_ref[...], preferred_element_type=jnp.float32)
    out_ref[...] = (grad * gelu_slope(pre + bias_ref[...])).astype(jnp.bfloat16)


def pre_backward(d_full, tokens, readers, bias):
    rows, width = tokens.shape
    depth = d_full.shape[1]
    step = 512
    skip = width // step
    return pl.pallas_call(
        pre_kernel,
        grid=(depth // step,),
        in_specs=[
            pl.BlockSpec((rows, depth), lambda i: (0, 0)),
            pl.BlockSpec((rows, width), lambda i: (0, 0)),
            pl.BlockSpec((step, depth), lambda i: (i + skip, 0)),
            pl.BlockSpec((width, step), lambda i: (0, i)),
            pl.BlockSpec((1, step), lambda i: (0, i)),
        ],
        out_specs=pl.BlockSpec((rows, step), lambda i: (0, i)),
        out_shape=shape_of((rows, depth), jnp.bfloat16),
        compiler_params=kernel_params(),
        name="pre_backward",
    )(d_full, tokens, readers, readers, bias[None])


def shards(
    patches,
    counts,
    cotangent,
    filters,
    filters_moment,
    filters_square,
    filters_average,
    vectors,
    vectors_moment,
    vectors_square,
    vectors_average,
    expand,
    expand_moment,
    expand_square,
    expand_average,
    project,
    project_moment,
    project_square,
    project_average,
    offsets,
    offsets_moment,
    offsets_square,
    offsets_average,
):
    inner = lax.axis_size("spot")
    wide = LINE * inner
    group = lax.axis_size("dp")
    devices = wide * group
    share = filters.shape[1]
    lanes = vectors.shape[2]
    columns = expand.shape[1]
    packed = jnp.concatenate(
        [
            filters.astype(jnp.bfloat16).reshape(4 * share, filters.shape[2]),
            pad_row(vectors.astype(jnp.bfloat16).reshape(1, -1), filters.shape[2]),
            pad_row(offsets.astype(jnp.bfloat16).reshape(1, -1), filters.shape[2]),
            jnp.zeros((14, filters.shape[2]), jnp.bfloat16),
        ]
    )
    spread = lax.all_gather(packed, ALL, axis=0)
    whole_filters = [
        spread[:, k * share : (k + 1) * share].reshape(devices * share, -1) for k in range(4)
    ]
    vec_full = (
        spread[:, 4 * share, : 30 * lanes]
        .reshape(devices, 2, 15, lanes)
        .transpose(1, 2, 0, 3)
        .reshape(2, 15, devices * lanes)
        .astype(jnp.float32)
    )
    full_offsets = (
        spread[:wide, 4 * share + 1, : 2 * columns]
        .reshape(wide, 2, columns)
        .transpose(1, 0, 2)
        .reshape(2, wide * columns)
        .astype(jnp.float32)
    )
    images = patches.shape[0]
    width = patches.shape[2]
    samples = counts.shape[0]
    image_index = jnp.arange(images, dtype=jnp.int32)
    owner = image_index // SLOTS
    slot = image_index % SLOTS
    matches = owner[:, None] == jnp.arange(samples, dtype=jnp.int32)[None, :]
    chosen = jnp.sum(jnp.where(matches, counts[None, :], 0), axis=1)
    live = (slot < chosen).astype(jnp.float32)
    rows = patches.reshape(images * GRID * GRID, width)
    pooled, first_saved = block_forward(
        rows, whole_filters[0], whole_filters[1], vec_full[0], GRID
    )
    tokens, second_saved = block_forward(
        pooled, whole_filters[2], whole_filters[3], vec_full[1], POOL, live
    )
    d_cols = cotangent.reshape(-1, columns)
    part = d_cols.shape[0] // wide
    readers = jnp.concatenate([expand.astype(jnp.bfloat16), project.astype(jnp.bfloat16)])
    readers = lax.all_gather(readers, WIDE, axis=1, tiled=True)
    d_full = lax.all_to_all(d_cols, WIDE, split_axis=0, concat_axis=1, tiled=True)
    g_out = jnp.sum(d_cols.astype(jnp.float32), axis=0)
    tokens_after, readers, d_late = lax.optimization_barrier((tokens, readers, d_cols))
    d_line = d_late.reshape(LINE, inner, part, columns).transpose(1, 0, 2, 3)
    d_line = lax.all_to_all(d_line, "spot", split_axis=0, concat_axis=0, tiled=True)
    d_line = d_line.reshape(inner, LINE * part, columns)
    full_expand = readers[:width]
    tokens_line = lax.all_gather(tokens_after, "line", axis=0, tiled=True)
    hidden_line = hidden_forward(tokens_line, readers, full_offsets[0])
    core = lax.axis_index("spot") % 2
    d_cores = d_line.reshape(inner // 2, 2, LINE * part, columns)

    def project_part(at):
        return lax.dot_general(
            held(pick(d_cores, at, 1)),
            hidden_line,
            (((1,), (0,)), ((), ())),
            preferred_element_type=jnp.float32,
        )

    d_pre = pre_backward(d_full, tokens, readers, full_offsets[0])
    theirs_sent = project_part(1 - core).astype(jnp.bfloat16)
    theirs = lax.ppermute(theirs_sent, "spot", [(i, i ^ 1) for i in range(inner)])
    g_project = project_part(core) + theirs.astype(jnp.float32)
    spot = lax.axis_index("spot") // 2
    step = 1
    while g_project.shape[0] > 1:
        halves = g_project.reshape(g_project.shape[0] // 2, 2, columns, -1)
        theirs_sent = pick(halves, 1 - spot % 2, 1).astype(jnp.bfloat16)
        step *= 2
        theirs = lax.ppermute(theirs_sent, "spot", [(i, i ^ step) for i in range(inner)])
        g_project = pick(halves, spot % 2, 1) + theirs.astype(jnp.float32)
        spot = spot // 2
    g_project = over_groups(g_project[0].astype(jnp.bfloat16), group)
    ones = jnp.ones((tokens.shape[0], 1), jnp.bfloat16)
    tokens_more = jnp.concatenate(
        [tokens, ones, jnp.zeros((tokens.shape[0], 15), jnp.bfloat16)], axis=1
    )
    g_expand_full = contract_rows(tokens_more, d_pre).astype(jnp.bfloat16)
    d_tokens = contract_cols(d_pre, full_expand)
    g_expand = lax.psum_scatter(g_expand_full, WIDE, scatter_dimension=1, tiled=True)
    g_expand = jnp.concatenate(
        [g_expand[: width + 1], g_out[None].astype(jnp.bfloat16), g_expand[width + 2 :]]
    )
    g_expand = over_groups(g_expand, group)
    g_offsets = g_expand[width : width + 2]
    g_expand = g_expand[:width]
    d_pooled, g_in_two, g_out_two, g_vec_two = block_backward(
        d_tokens, second_saved, whole_filters[2], whole_filters[3], vec_full[1], POOL, live
    )
    d_pooled, theirs_sent = lax.optimization_barrier((d_pooled, theirs_sent))
    d_rows, g_in_one, g_out_one, g_vec_one = block_backward(
        d_pooled, first_saved, whole_filters[0], whole_filters[1], vec_full[0], GRID
    )
    hidden_line, d_rows = lax.optimization_barrier((hidden_line, d_rows))
    at = lax.axis_index("line") * inner * columns
    project_line = lax.dynamic_slice(
        readers, (width, at), (readers.shape[0] - width, inner * columns)
    )
    offset_line = lax.dynamic_slice_in_dim(full_offsets[1], at, inner * columns, 0)
    out_line = (
        jnp.dot(hidden_line, project_line, preferred_element_type=jnp.float32) + offset_line
    ).astype(jnp.bfloat16)
    out_line = out_line.reshape(LINE * part, inner, columns).transpose(1, 0, 2)
    out_cols = lax.all_to_all(out_line, "spot", split_axis=0, concat_axis=0, tiled=True)
    readout = (
        out_cols.reshape(inner, LINE, part, columns)
        .transpose(1, 0, 2, 3)
        .reshape(-1, POOL * POOL, columns)
    )
    patch_gradient = d_rows.reshape(images, GRID * GRID, width)
    g_two = reduce_block(g_in_two, g_out_two, g_vec_two, devices)
    g_two = spread_reduce(g_two)
    g_one = reduce_block(g_in_one, g_out_one, g_vec_one, devices)
    g_one = spread_reduce(g_one)
    g_filters = jnp.stack(
        [g_one[:share], g_one[share : 2 * share], g_two[:share], g_two[share : 2 * share]]
    ).astype(jnp.float32)
    g_vectors = jnp.stack(
        [g_one[2 * share, : 15 * lanes], g_two[2 * share, : 15 * lanes]]
    ).reshape(2, 15, lanes).astype(jnp.float32)
    filters_out = adamw(
        filters, g_filters, filters_moment, filters_square, filters_average, 0.03, 0.05
    )
    vectors_out = adamw(
        vectors, g_vectors, vectors_moment, vectors_square, vectors_average, 0.3, 0.0
    )
    expand_out = adamw(expand, g_expand, expand_moment, expand_square, expand_average, 0.03, 0.05)
    project_out = adamw_turned(
        project, g_project, project_moment, project_square, project_average, 0.016, 0.05
    )
    offsets_out = adamw(
        offsets, g_offsets, offsets_moment, offsets_square, offsets_average, 0.1, 0.0
    )
    return (
        readout,
        patch_gradient,
        filters_out[0],
        filters_out[1],
        filters_out[2],
        filters_out[3],
        filters_out[4],
        vectors_out[0],
        vectors_out[1],
        vectors_out[2],
        vectors_out[3],
        vectors_out[4],
        expand_out[0],
        expand_out[1],
        expand_out[2],
        expand_out[3],
        expand_out[4],
        project_out[0],
        project_out[1],
        project_out[2],
        project_out[3],
        project_out[4],
        offsets_out[0],
        offsets_out[1],
        offsets_out[2],
        offsets_out[3],
        offsets_out[4],
    )


def solution(mesh):
    in_specs = (
        P(ALL, None, None),
        P(ALL),
        P("dp", None, WIDE),
        P(None, ALL, None),
        P(None, ALL, None),
        P(None, ALL, None),
        P(None, ALL, None),
        P(None, None, ALL),
        P(None, None, ALL),
        P(None, None, ALL),
        P(None, None, ALL),
        P(None, WIDE),
        P(None, WIDE),
        P(None, WIDE),
        P(None, WIDE),
        P(None, WIDE),
        P(None, WIDE),
        P(None, WIDE),
        P(None, WIDE),
        P(None, WIDE),
        P(None, WIDE),
        P(None, WIDE),
        P(None, WIDE),
    )
    out_specs = (
        P("dp", None, WIDE),
        P(ALL, None, None),
        P(None, ALL, None),
        P(None, ALL, None),
        P(None, ALL, None),
        P(None, ALL, None),
        P(None, ALL, None),
        P(None, None, ALL),
        P(None, None, ALL),
        P(None, None, ALL),
        P(None, None, ALL),
        P(None, None, ALL),
        P(None, WIDE),
        P(None, WIDE),
        P(None, WIDE),
        P(None, WIDE),
        P(None, WIDE),
        P(None, WIDE),
        P(None, WIDE),
        P(None, WIDE),
        P(None, WIDE),
        P(None, WIDE),
        P(None, WIDE),
        P(None, WIDE),
        P(None, WIDE),
        P(None, WIDE),
        P(None, WIDE),
    )
    devices = mesh.devices
    lines = Mesh(
        devices.reshape(devices.shape[0], LINE, devices.shape[1] // LINE), ("dp", "line", "spot")
    )
    return jax.shard_map(shards, mesh=lines, in_specs=in_specs, out_specs=out_specs, check_vma=False)
```

```python
import math
from functools import partial

import jax
import jax.numpy as jnp
from jax import lax
from jax.experimental import pallas as pl
from jax.experimental.pallas import tpu as pltpu
from jax.sharding import Mesh
from jax.sharding import PartitionSpec as P

GRID = 24
POOL = 12
SLOTS = 4
STEP = 3
LINE = 4
WIDE = ("line", "spot")
ALL = ("dp", "line", "spot")


beta_one = 0.5
beta_two = 0.5
adam_eps = 1e-08
ema_keep = 0.75
norm_eps = 1e-06


def contract_rows(left, right):
    return lax.dot_general(
        left, right, (((0,), (0,)), ((), ())), preferred_element_type=jnp.float32
    )


def contract_cols(left, right):
    return lax.dot_general(
        left, right, (((1,), (1,)), ((), ())), preferred_element_type=jnp.float32
    )


CHUNK = 48
LANE = 128


def shape_of(shape, kind):
    return jax.ShapeDtypeStruct(shape, kind)


def sigmoid(value):
    return 0.5 * jnp.tanh(0.5 * value) + 0.5


def fold_rows(value):
    return jnp.sum(value.reshape(value.shape[0] // 8, 8, value.shape[1]), axis=0)


def row_span(k, size):
    return pl.ds(pl.multiple_of(k * size, 16), size)


def lane_span(j):
    return pl.ds(j * LANE, LANE)


def row_total(parts):
    total = parts[0]
    for part in parts[1:]:
        total = total + part
    return jnp.sum(total, axis=1, keepdims=True)


def normalize(read, norm_ref, scale_ref, span, finish):
    width = norm_ref.shape[1]
    spans = [lane_span(j) for j in range(width // LANE)]
    center = row_total([read(lanes) for lanes in spans]) * (1.0 / width)
    spread = row_total([jnp.square(read(lanes) - center) for lanes in spans]) * (1.0 / width)
    scale = lax.rsqrt(spread + norm_eps)
    scale_ref[span, :] = jnp.broadcast_to(scale, (span.size, LANE))
    for lanes in spans:
        unit = (read(lanes) - center) * scale
        norm_ref[span, lanes] = unit
        finish(lanes, unit)


def shift_rows(value, amount, mask):
    return pltpu.roll(value, amount % value.shape[0], 0) * mask


def masks_for(side, rows):
    cell = jnp.arange(rows, dtype=jnp.int32)
    x, y = cell % side, (cell // side) % side
    flags = jnp.stack([x > 0, x < side - 1, y > 0, y < side - 1]).astype(jnp.float32)
    return jnp.broadcast_to(flags[:, :, None], (4, rows, LANE))


def conv_block(above, level, below, taps, mask_ref):
    columns = [
        taps[c] * above + taps[3 + c] * level + taps[6 + c] * below for c in range(3)
    ]
    return (
        columns[1]
        + shift_rows(columns[0], 1, mask_ref[0])
        + shift_rows(columns[2], -1, mask_ref[1])
    )


def taps_at(vec_ref, lanes):
    return [vec_ref[k : k + 1, lanes] for k in range(9)]


def forward_kernel(side, *refs):
    pooled = side == GRID
    if pooled:
        x_ref, in_ref, out_ref, vec_ref, mask_ref, pool_ref = refs[:6]
        n1_ref, n2_ref, n3_ref, r1_ref, r2_ref, r3_ref, b_ref, y_ref = refs[6:14]
        lin_ref, act_ref, hi_ref, lo_ref = refs[14:]
    else:
        live_ref, x_ref, in_ref, out_ref, vec_ref, mask_ref = refs[:6]
        n1_ref, n2_ref, n3_ref, r1_ref, r2_ref, r3_ref, b_ref, y_ref = refs[6:14]
        lin_ref, act_ref = refs[14:]
    rows, width = x_ref.shape
    count = rows // CHUNK
    edge = side if pooled else 0
    lin_ref[...] = jnp.dot(x_ref[...], in_ref[...], preferred_element_type=jnp.float32)
    if pooled:
        act_ref[0:side, :] = jnp.zeros((side, width), jnp.float32)
        act_ref[rows + side : rows + 2 * side, :] = jnp.zeros((side, width), jnp.float32)

    @pl.loop(0, count)
    def _(k):
        span = row_span(k, CHUNK)
        above = pl.ds(pl.multiple_of(k * CHUNK + edge, 8), CHUNK)

        def finish(lanes, unit):
            value = unit * vec_ref[9:10, lanes] + vec_ref[10:11, lanes]
            act_ref[above, lanes] = value * sigmoid(value)

        normalize(lambda lanes: lin_ref[span, lanes], n1_ref, r1_ref, span, finish)

    if pooled:

        @pl.loop(0, count)
        def _(k):
            for j in range(width // LANE):
                lanes = lane_span(j)
                near = [
                    act_ref[pl.ds(pl.multiple_of(k * CHUNK + r * side, 8), CHUNK), lanes]
                    for r in range(3)
                ]
                lin_ref[row_span(k, CHUNK), lanes] = conv_block(
                    near[0], near[1], near[2], taps_at(vec_ref, lanes), mask_ref
                )
    else:
        cells = side * side

        @pl.loop(0, rows // cells)
        def _(k):
            for j in range(width // LANE):
                lanes = lane_span(j)
                level = act_ref[row_span(k, cells), lanes]
                lin_ref[row_span(k, cells), lanes] = conv_block(
                    shift_rows(level, side, mask_ref[2]),
                    level,
                    shift_rows(level, -side, mask_ref[3]),
                    taps_at(vec_ref, lanes),
                    mask_ref,
                )

    @pl.loop(0, count)
    def _(k):
        span = row_span(k, CHUNK)

        def finish(lanes, unit):
            value = unit * vec_ref[11:12, lanes] + vec_ref[12:13, lanes]
            b_ref[span, lanes] = (value * sigmoid(value)).astype(jnp.bfloat16)

        normalize(lambda lanes: lin_ref[span, lanes], n2_ref, r2_ref, span, finish)

    lin_ref[...] = jnp.dot(b_ref[...], out_ref[...], preferred_element_type=jnp.float32)

    @pl.loop(0, count)
    def _(k):
        span = row_span(k, CHUNK)
        if not pooled:
            scale = live_ref[k * CHUNK // (side * side)]

        def finish(lanes, unit):
            value = (
                x_ref[span, lanes].astype(jnp.float32)
                + unit * vec_ref[13:14, lanes]
                + vec_ref[14:15, lanes]
            )
            value = value * sigmoid(value)
            if pooled:
                high = value.astype(jnp.bfloat16)
                hi_ref[span, lanes] = high
                lo_ref[span, lanes] = (value - high.astype(jnp.float32)).astype(jnp.bfloat16)
            else:
                y_ref[span, lanes] = (value * scale).astype(jnp.bfloat16)

        normalize(lambda lanes: lin_ref[span, lanes], n3_ref, r3_ref, span, finish)

    if pooled:
        y_ref[...] = (
            jnp.dot(pool_ref[...], hi_ref[...], preferred_element_type=jnp.float32)
            + jnp.dot(pool_ref[...], lo_ref[...], preferred_element_type=jnp.float32)
        ).astype(jnp.bfloat16)


def backward_kernel(side, *refs):
    pooled = side == GRID
    if pooled:
        up_ref, d_ref, x_ref, in_ref, out_ref, vec_ref, mask_ref = refs[:7]
    else:
        live_ref, d_ref, x_ref, in_ref, out_ref, vec_ref, mask_ref = refs[:7]
    n1_ref, n2_ref, n3_ref, r1_ref, r2_ref, r3_ref = refs[7:13]
    dx_ref, da_ref, dc_ref, sum_ref = refs[13:17]
    res_ref, mix_ref, act_ref = refs[17:20]
    rows, width = x_ref.shape
    count = rows // CHUNK
    edge = side if pooled else 0
    spans = [lane_span(j) for j in range(width // LANE)]

    @pl.when(pl.program_id(0) == 0)
    def _():
        sum_ref[...] = jnp.zeros(sum_ref.shape, jnp.float32)

    def add_sum(k, lanes, value):
        sum_ref[8 * k : 8 * k + 8, lanes] += fold_rows(value)

    if pooled:
        grads = d_ref[...]
        high = grads.astype(jnp.bfloat16)
        low = (grads - high.astype(jnp.float32)).astype(jnp.bfloat16)
        res_ref[...] = jnp.dot(
            up_ref[...], high, preferred_element_type=jnp.float32
        ) + jnp.dot(up_ref[...], low, preferred_element_type=jnp.float32)

    def norm_back(unit_ref, scale_ref, span, gain, read_grad, store):
        first, second = [], []
        for lanes in spans:
            grad = read_grad(lanes) * vec_ref[gain : gain + 1, lanes]
            first.append(grad)
            second.append(grad * unit_ref[span, lanes])
        mean_grad = row_total(first) * (1.0 / width)
        mean_unit = row_total(second) * (1.0 / width)
        for lanes in spans:
            grad = read_grad(lanes) * vec_ref[gain : gain + 1, lanes]
            store(
                lanes,
                scale_ref[span, :]
                * (grad - mean_grad - unit_ref[span, lanes] * mean_unit),
            )

    @pl.loop(0, count)
    def _(k):
        span = row_span(k, CHUNK)
        if not pooled:
            scale = live_ref[k * CHUNK // (side * side)]
        for lanes in spans:
            unit = n3_ref[span, lanes]
            value = (
                x_ref[span, lanes].astype(jnp.float32)
                + unit * vec_ref[13:14, lanes]
                + vec_ref[14:15, lanes]
            )
            gate = sigmoid(value)
            grad = res_ref[span, lanes] if pooled else d_ref[span, lanes] * scale
            grad = grad * (gate * (1.0 + value * (1.0 - gate)))
            res_ref[span, lanes] = grad
            add_sum(13, lanes, grad * unit)
            add_sum(14, lanes, grad)

        def store(lanes, value):
            dc_ref[span, lanes] = value.astype(jnp.bfloat16)

        norm_back(n3_ref, r3_ref, span, 13, lambda lanes: res_ref[span, lanes], store)

    if pooled:
        mix_ref[0:side, :] = jnp.zeros((side, width), jnp.float32)
        mix_ref[rows + side : rows + 2 * side, :] = jnp.zeros((side, width), jnp.float32)
    mix_ref[edge : rows + edge, :] = contract_cols(dc_ref[...], out_ref[...])

    @pl.loop(0, count)
    def _(k):
        span = row_span(k, CHUNK)
        at = pl.ds(pl.multiple_of(k * CHUNK + edge, 8), CHUNK)
        for lanes in spans:
            unit = n2_ref[span, lanes]
            value = unit * vec_ref[11:12, lanes] + vec_ref[12:13, lanes]
            gate = sigmoid(value)
            grad = mix_ref[at, lanes] * (gate * (1.0 + value * (1.0 - gate)))
            mix_ref[at, lanes] = grad
            add_sum(11, lanes, grad * unit)
            add_sum(12, lanes, grad)

        def store(lanes, value):
            mix_ref[at, lanes] = value

        norm_back(n2_ref, r2_ref, span, 11, lambda lanes: mix_ref[at, lanes], store)

    size = CHUNK if pooled else side * side

    @pl.loop(0, rows // size)
    def _(k):
        span = row_span(k, size)
        for lanes in spans:
            if pooled:
                near = [
                    mix_ref[pl.ds(pl.multiple_of(k * size + (2 - r) * side, 8), size), lanes]
                    for r in range(3)
                ]
            else:
                level = mix_ref[span, lanes]
                near = [
                    shift_rows(level, -side, mask_ref[3]),
                    level,
                    shift_rows(level, side, mask_ref[2]),
                ]
            taps = taps_at(vec_ref, lanes)
            mixed = [
                taps[c] * near[0] + taps[3 + c] * near[1] + taps[6 + c] * near[2]
                for c in range(3)
            ]
            grad = (
                mixed[1]
                + shift_rows(mixed[0], -1, mask_ref[1])
                + shift_rows(mixed[2], 1, mask_ref[0])
            )
            unit = n1_ref[span, lanes]
            value = unit * vec_ref[9:10, lanes] + vec_ref[10:11, lanes]
            gate = sigmoid(value)
            active = value * gate
            sides = [
                shift_rows(active, 1, mask_ref[0]),
                active,
                shift_rows(active, -1, mask_ref[1]),
            ]
            for r in range(3):
                for c in range(3):
                    add_sum(3 * r + c, lanes, sides[c] * near[r])
            grad = grad * (gate * (1.0 + value * (1.0 - gate)))
            act_ref[span, lanes] = grad
            add_sum(9, lanes, grad * unit)
            add_sum(10, lanes, grad)

    @pl.loop(0, count)
    def _(k):
        span = row_span(k, CHUNK)

        def store(lanes, value):
            da_ref[span, lanes] = value.astype(jnp.bfloat16)

        norm_back(n1_ref, r1_ref, span, 9, lambda lanes: act_ref[span, lanes], store)

    step = 256
    for j in range(width // step):
        dx_ref[:, j * step : (j + 1) * step] = (
            res_ref[:, j * step : (j + 1) * step]
            + contract_cols(da_ref[...], in_ref[j * step : (j + 1) * step, :])
        ).astype(dx_ref.dtype)


def pool_matrix():
    cell = jnp.arange(GRID * GRID, dtype=jnp.int32)
    home = (cell // GRID // 2) * POOL + (cell % GRID) // 2
    spot = jnp.arange(POOL * POOL, dtype=jnp.int32)
    return jnp.where(home[None, :] == spot[:, None], 0.25, 0.0).astype(jnp.bfloat16)


def block_specs(side, rows, width):
    whole = lambda shape: pl.BlockSpec(shape, lambda i: (0,) * len(shape))
    part = lambda cells, lanes: pl.BlockSpec((cells, lanes), lambda i: (i, 0))
    size = side * side if side == GRID else rows
    return whole, part, size


def kernel_params(axes=1):
    return pltpu.CompilerParams(
        dimension_semantics=("arbitrary",) * axes, vmem_limit_bytes=60 * 1024 * 1024
    )


def block_forward(rows, w_in, w_out, vecs, side, live=None):
    total, width = rows.shape
    whole, part, size = block_specs(side, total, width)
    pooled = side == GRID
    mask_rows = CHUNK if pooled else side * side
    vecs = jnp.pad(vecs, ((0, 1), (0, 0)))
    masks = masks_for(side, mask_rows)
    norm = shape_of((total, width), jnp.float32)
    scale = shape_of((total, LANE), jnp.float32)
    out_cells = POOL * POOL if pooled else size
    operands = [rows, w_in, w_out, vecs, masks]
    in_specs = [
        part(size, width),
        whole(w_in.shape),
        whole(w_out.shape),
        whole(vecs.shape),
        whole(masks.shape),
    ]
    scratch = [
        pltpu.VMEM((size, width), jnp.float32),
        pltpu.VMEM((size + 2 * side, width) if pooled else (size, width), jnp.float32),
    ]
    if pooled:
        operands.append(pool_matrix())
        in_specs.append(whole((POOL * POOL, GRID * GRID)))
        scratch += [pltpu.VMEM((size, width), jnp.bfloat16)] * 2
    else:
        operands.insert(0, live)
        in_specs.insert(0, pl.BlockSpec(memory_space=pltpu.SMEM))
    outs = pl.pallas_call(
        partial(forward_kernel, side),
        grid=(total // size,),
        in_specs=in_specs,
        out_specs=[part(size, width)] * 3
        + [part(size, LANE)] * 3
        + [part(size, width), part(out_cells, width)],
        out_shape=[norm] * 3
        + [scale] * 3
        + [
            shape_of((total, width), jnp.bfloat16),
            shape_of((total // size * out_cells, width), jnp.bfloat16),
        ],
        scratch_shapes=scratch,
        compiler_params=kernel_params(),
        name="block_forward_" + str(side),
    )(*operands)
    return outs[7], (rows, outs[6], tuple(outs[:6]))


def block_backward(d_result, saved, w_in, w_out, vecs, side, live=None):
    rows, narrow, kept = saved
    total, width = rows.shape
    whole, part, size = block_specs(side, total, width)
    pooled = side == GRID
    mask_rows = CHUNK if pooled else side * side
    vecs = jnp.pad(vecs, ((0, 1), (0, 0)))
    masks = masks_for(side, mask_rows)
    in_cells = POOL * POOL if pooled else size
    if pooled:
        first = pool_matrix().T
        first_spec = whole(first.shape)
    else:
        first = live
        first_spec = pl.BlockSpec(memory_space=pltpu.SMEM)
    low = shape_of((total, width), jnp.bfloat16)
    dx, da, dc, sums = pl.pallas_call(
        partial(backward_kernel, side),
        grid=(total // size,),
        in_specs=[
            first_spec,
            part(in_cells, width),
            part(size, width),
            whole(w_in.shape),
            whole(w_out.shape),
            whole(vecs.shape),
            whole(masks.shape),
        ]
        + [part(size, width)] * 3
        + [part(size, LANE)] * 3,
        out_specs=[part(size, width)] * 3 + [whole((128, width))],
        out_shape=[
            shape_of((total, width), jnp.bfloat16 if pooled else jnp.float32),
            low,
            low,
            shape_of((128, width), jnp.float32),
        ],
        scratch_shapes=[
            pltpu.VMEM((size, width), jnp.float32),
            pltpu.VMEM((size + 2 * side, width) if pooled else (size, width), jnp.float32),
            pltpu.VMEM((size, width), jnp.float32),
        ],
        compiler_params=kernel_params(),
        name="block_backward_" + str(side),
    )(first, d_result, rows, w_in, w_out, vecs, masks, *kept)
    grad_out = contract_rows(narrow, dc)
    grad_in = contract_rows(rows, da)
    grad_vecs = jnp.sum(sums[:120].reshape(15, 8, width), axis=1)
    return dx, grad_in, grad_out, grad_vecs


def adamw(weight, grad, moment, square, average, rate, decay):
    momentum = beta_one * moment + (1.0 - beta_one) * grad
    variance = beta_two * square + (1.0 - beta_two) * grad * grad
    scaled_m = momentum / (1.0 - beta_one**STEP)
    scaled_v = variance / (1.0 - beta_two**STEP)
    updated = weight - rate * (scaled_m / (jnp.sqrt(scaled_v) + adam_eps) + decay * weight)
    smoothed = ema_keep * average + (1.0 - ema_keep) * updated
    return (updated, momentum, variance, smoothed, updated.astype(jnp.bfloat16))


def pad_row(row, width):
    return jnp.pad(row, ((0, 0), (0, width - row.shape[1])))


def ring_order(chips):
    inner = chips // LINE
    cells = [(o, 0) for o in range(LINE)]
    for turn, o in enumerate(reversed(range(LINE))):
        line = list(range(1, inner))
        cells += [(o, i) for i in (line if turn % 2 == 0 else line[::-1])]
    return [o * inner + i for o, i in cells]


def ring_gather(value, inner, group):
    chips = LINE * inner // 2
    ring = ring_order(chips)
    back = sorted(range(chips), key=lambda place: ring[place])
    index = lax.axis_index(WIDE)
    core = index % 2
    place = jnp.asarray(back, jnp.int32)[index // 2]
    turn = 1 - 2 * core
    pairs = []
    for r in range(chips):
        ahead, behind = ring[(r + 1) % chips], ring[(r - 1) % chips]
        pairs += [(ring[r] * 2, ahead * 2), (ring[r] * 2 + 1, behind * 2 + 1)]
    spots = jnp.asarray(ring, jnp.int32)
    held_all = jnp.zeros((chips,) + value.shape, value.dtype)
    for s in range(chips):
        if s:
            value = lax.ppermute(value, WIDE, pairs)
        if s == chips // 2:
            middle = value
        spot = spots[(place - turn * s) % chips]
        held_all = lax.dynamic_update_index_in_dim(held_all, value, spot, 0)
    if group == 2:
        other = lax.ppermute(held_all, "dp", [(0, 1), (1, 0)])
        first = lax.axis_index("dp") == 0
        planes = jnp.stack(
            [jnp.where(first, held_all, other), jnp.where(first, other, held_all)]
        )
    else:
        planes = lax.all_gather(held_all, "dp", axis=0)
    other = lax.ppermute(planes, "spot", [(i, i ^ 1) for i in range(inner)])
    first = core == 0
    planes = jnp.stack([jnp.where(first, planes, other), jnp.where(first, other, planes)], axis=2)
    return planes, middle


def swap_groups(value, group):
    return lax.ppermute(value, "dp", [(i, i ^ 1) for i in range(group)])


def over_groups(value, group):
    if group == 2:
        other = lax.ppermute(value, "dp", [(0, 1), (1, 0)])
        return value.astype(jnp.float32) + other.astype(jnp.float32)
    return lax.psum(value, "dp").astype(jnp.float32)


def reduce_block(grad_in, grad_out, grad_vecs, devices):
    width = grad_in.shape[1]
    share = width // devices
    rows = [
        grad_in.astype(jnp.bfloat16).reshape(devices, share, width),
        grad_out.astype(jnp.bfloat16).reshape(devices, share, width),
        jnp.pad(
            grad_vecs.astype(jnp.bfloat16)
            .reshape(15, devices, share)
            .transpose(1, 0, 2)
            .reshape(devices, 1, 15 * share),
            ((0, 0), (0, 15), (0, width - 15 * share)),
        ),
    ]
    return jnp.concatenate(rows, axis=1)


def pick(value, at, axis):
    return lax.dynamic_index_in_dim(value, at, axis, False)


def after(value, *others):
    return lax.optimization_barrier((value,) + others)[0]


def spread_reduce(blocks, works):
    count = blocks.shape[0]
    bits = count.bit_length() - 1
    order = [0, 1] + list(range(bits - 1, 1, -1))
    me = lax.axis_index(ALL)
    blocks = blocks.reshape((2,) * bits + blocks.shape[1:])
    left = list(range(bits))[::-1]
    for stage, bit in enumerate(order):
        axis = left.index(bit)
        left.pop(axis)
        mine = (me >> bit) & 1
        pairs = [(i, i ^ (1 << bit)) for i in range(count)]
        sent = pick(blocks, 1 - mine, axis)
        theirs = lax.ppermute(sent, ALL, pairs)
        if stage < len(works):
            theirs = after(theirs, works[stage](blocks))
        blocks = (
            pick(blocks, mine, axis).astype(jnp.float32) + theirs.astype(jnp.float32)
        ).astype(jnp.bfloat16)
    return blocks


def held(value):
    return lax.optimization_barrier(value)


def gelu_slope(value):
    return 0.5 * (1.0 + lax.erf(value * (0.5**0.5))) + value * jnp.exp(-0.5 * value * value) * (
        0.5 / math.pi
    ) ** 0.5


def hidden_kernel(tokens_ref, expand_ref, bias_ref, out_ref):
    pre = jnp.dot(tokens_ref[...], expand_ref[...], preferred_element_type=jnp.float32)
    pre = pre + bias_ref[...]
    out_ref[...] = (0.5 * pre * (1.0 + lax.erf(pre * (0.5**0.5)))).astype(jnp.bfloat16)


def hidden_forward(tokens, readers, bias, half):
    total, width = tokens.shape
    depth = readers.shape[1] // 2
    rows, step = total // LINE, 512
    skip = half * depth // step
    return pl.pallas_call(
        hidden_kernel,
        grid=(depth // step, LINE),
        in_specs=[
            pl.BlockSpec((rows, width), lambda j, i: (i, 0)),
            pl.BlockSpec((width, step), lambda j, i: (0, j + skip)),
            pl.BlockSpec((1, step), lambda j, i: (0, j + skip)),
        ],
        out_specs=pl.BlockSpec((rows, step), lambda j, i: (i, j)),
        out_shape=shape_of((total, depth), jnp.bfloat16),
        compiler_params=kernel_params(2),
        name="hidden_forward",
    )(tokens, readers, bias[None])


def adamw_kernel(rate, decay, grad_ref, *refs):
    old, new = refs[:4], refs[4:]
    results = adamw(old[0][...], grad_ref[...].T, *[ref[...] for ref in old[1:]], rate, decay)
    for ref, result in zip(new, results):
        ref[...] = result


def adamw_turned(weight, grad, moment, square, average, rate, decay):
    depth, columns = weight.shape
    step = 512
    part = pl.BlockSpec((step, columns), lambda i: (i, 0))
    return pl.pallas_call(
        partial(adamw_kernel, rate, decay),
        grid=(depth // step,),
        in_specs=[pl.BlockSpec((columns, step), lambda i: (0, i))] + [part] * 4,
        out_specs=[part] * 5,
        out_shape=[shape_of(weight.shape, jnp.float32)] * 4
        + [shape_of(weight.shape, jnp.bfloat16)],
        compiler_params=kernel_params(),
        name="adamw_turned",
    )(grad, weight, moment, square, average)


def pre_kernel(counts, at_ref, d_ref, tokens_ref, *refs):
    sources, (expand_ref, bias_ref, out_ref) = refs[: len(counts)], refs[len(counts) :]
    pre = jnp.dot(tokens_ref[...], expand_ref[...], preferred_element_type=jnp.float32)
    slope = gelu_slope(pre + bias_ref[...])
    index = pl.program_id(0)
    start = 0
    for count, source in zip(counts, sources):

        @pl.when((index >= start) & (index < start + count))
        def _(source=source):
            grad = contract_cols(d_ref[...], source[...])
            out_ref[...] = (grad * slope).astype(jnp.bfloat16)

        start += count


def pre_backward(d_full, tokens, shared, bias, pieces):
    rows, width = tokens.shape
    depth = d_full.shape[1]
    step = 512
    counts = [size // step for _, _, _, size in pieces]
    order = jnp.concatenate(
        [
            jnp.asarray(start // step, jnp.int32) + jnp.arange(size // step, dtype=jnp.int32)
            for _, _, start, size in pieces
        ]
    )
    specs = []
    first = 0
    for (source, skip, _, size), count in zip(pieces, counts):
        low, high = skip // step, skip // step + count - 1
        specs.append(
            pl.BlockSpec(
                (step, depth),
                lambda i, at, low=low, high=high, first=first: (
                    jnp.clip(i - first + low, low, high),
                    0,
                ),
            )
        )
        first += count
    return pl.pallas_call(
        partial(pre_kernel, counts),
        grid_spec=pltpu.PrefetchScalarGridSpec(
            num_scalar_prefetch=1,
            grid=(depth // step,),
            in_specs=[
                pl.BlockSpec((rows, depth), lambda i, at: (0, 0)),
                pl.BlockSpec((rows, width), lambda i, at: (0, 0)),
            ]
            + specs
            + [
                pl.BlockSpec((width, step), lambda i, at: (0, at[i])),
                pl.BlockSpec((1, step), lambda i, at: (0, at[i])),
            ],
            out_specs=pl.BlockSpec((rows, step), lambda i, at: (0, at[i])),
        ),
        out_shape=shape_of((rows, depth), jnp.bfloat16),
        compiler_params=kernel_params(),
        name="pre_backward",
    )(order, d_full, tokens, *[piece[0] for piece in pieces], shared, bias[None])


def shards(
    patches,
    counts,
    cotangent,
    filters,
    filters_moment,
    filters_square,
    filters_average,
    vectors,
    vectors_moment,
    vectors_square,
    vectors_average,
    expand,
    expand_moment,
    expand_square,
    expand_average,
    project,
    project_moment,
    project_square,
    project_average,
    offsets,
    offsets_moment,
    offsets_square,
    offsets_average,
):
    inner = lax.axis_size("spot")
    wide = LINE * inner
    group = lax.axis_size("dp")
    devices = wide * group
    share = filters.shape[1]
    lanes = vectors.shape[2]
    columns = expand.shape[1]
    packed = jnp.concatenate(
        [
            filters.astype(jnp.bfloat16).reshape(4 * share, filters.shape[2]),
            pad_row(vectors.astype(jnp.bfloat16).reshape(1, -1), filters.shape[2]),
            pad_row(offsets.astype(jnp.bfloat16).reshape(1, -1), filters.shape[2]),
            jnp.zeros((14, filters.shape[2]), jnp.bfloat16),
        ]
    )
    spread, middle = ring_gather(packed, inner, group)
    whole_filters = [
        spread[:, :, :, k * share : (k + 1) * share].reshape(devices * share, -1)
        for k in range(4)
    ]
    spread = spread[:, :, :, 4 * share : 4 * share + 2].reshape(devices, 2, -1)
    vec_full = (
        spread[:, 0, : 30 * lanes]
        .reshape(devices, 2, 15, lanes)
        .transpose(1, 2, 0, 3)
        .reshape(2, 15, devices * lanes)
        .astype(jnp.float32)
    )
    full_offsets = (
        spread[:wide, 1, : 2 * columns]
        .reshape(wide, 2, columns)
        .transpose(1, 0, 2)
        .reshape(2, wide * columns)
        .astype(jnp.float32)
    )
    images = patches.shape[0]
    width = patches.shape[2]
    samples = counts.shape[0]
    image_index = jnp.arange(images, dtype=jnp.int32)
    owner = image_index // SLOTS
    slot = image_index % SLOTS
    matches = owner[:, None] == jnp.arange(samples, dtype=jnp.int32)[None, :]
    chosen = jnp.sum(jnp.where(matches, counts[None, :], 0), axis=1)
    live = (slot < chosen).astype(jnp.float32)
    rows = patches.reshape(images * GRID * GRID, width)
    d_cols = cotangent.reshape(-1, columns)
    part = d_cols.shape[0] // wide
    plane = lax.axis_index("dp") % 2
    swap = [(i, i ^ 1) for i in range(inner)]
    cross = [(i, i ^ 1) for i in range(group)]
    core = lax.axis_index("spot") % 2
    depth = project.shape[0]
    quarter = depth // 4
    project_low = project.astype(jnp.bfloat16)
    own = lax.dynamic_slice_in_dim(project_low, depth // 2 + plane * quarter, quarter, 0)
    shared = jnp.concatenate([expand.astype(jnp.bfloat16), project_low[: depth // 2]])
    own = lax.all_gather(own, WIDE, axis=1, tiled=True)
    shared = lax.all_gather(after(shared, middle), WIDE, axis=1, tiled=True)
    near = pick(after(own, whole_filters[0]).reshape(2, quarter // 2, -1), core, 0)
    near = lax.ppermute(near, "dp", cross)
    pooled, first_saved = block_forward(
        rows, whole_filters[0], whole_filters[1], vec_full[0], GRID
    )
    tokens, second_saved = block_forward(
        pooled, whole_filters[2], whole_filters[3], vec_full[1], POOL, live
    )
    near = after(near, tokens)
    far = lax.ppermute(near, "spot", swap)
    d_full = lax.all_to_all(d_cols, WIDE, split_axis=0, concat_axis=0, tiled=True)
    d_full = after(d_full, whole_filters[0]).reshape(wide, part, columns)
    d_full = d_full.transpose(1, 0, 2).reshape(part, wide * columns)
    g_out = jnp.sum(d_cols.astype(jnp.float32), axis=0)
    d_line = d_cols.reshape(LINE, inner, part, columns).transpose(1, 0, 2, 3)
    tokens_after, shared, d_line, d_full, g_out = lax.optimization_barrier(
        (tokens, shared, d_line, d_full, g_out)
    )
    full_expand = shared[:width]
    tokens_line = lax.all_gather(tokens_after, "line", axis=0, tiled=True)
    d_line = lax.all_to_all(d_line, "spot", split_axis=0, concat_axis=0, tiled=True)
    d_line = d_line.reshape(inner, LINE * part, columns)
    d_cores = d_line.reshape(inner // 2, 2, LINE * part, columns)
    near_at = depth // 2 + (1 - plane) * quarter + core * (quarter // 2)
    far_at = depth // 2 + (1 - plane) * quarter + (1 - core) * (quarter // 2)
    d_pre = pre_backward(
        d_full,
        tokens,
        shared,
        full_offsets[0],
        [
            (shared, width, 0, depth // 2),
            (own, 0, depth // 2 + plane * quarter, quarter),
            (near, 0, near_at, quarter // 2),
            (far, 0, far_at, quarter // 2),
        ],
    )
    d_tokens = contract_cols(d_pre, full_expand)
    d_pooled, g_in_two, g_out_two, g_vec_two = block_backward(
        d_tokens, second_saved, whole_filters[2], whole_filters[3], vec_full[1], POOL, live
    )
    g_two = reduce_block(g_in_two, g_out_two, g_vec_two, devices)
    d_pooled, g_two, d_theirs, d_mine = held(
        (d_pooled, g_two, pick(d_cores, 1 - core, 1), pick(d_cores, core, 1))
    )
    g_two = lax.psum_scatter(g_two, ALL, scatter_dimension=0, tiled=False)
    d_rows, g_in_one, g_out_one, g_vec_one = block_backward(
        d_pooled, first_saved, whole_filters[0], whole_filters[1], vec_full[0], GRID
    )
    patch_gradient = d_rows.reshape(images, GRID * GRID, width)
    g_one = reduce_block(g_in_one, g_out_one, g_vec_one, devices)
    got = {}

    def expand_work(done):
        ones = jnp.ones((tokens.shape[0], 1), jnp.bfloat16)
        more = [after(tokens, done), ones, jnp.zeros((tokens.shape[0], 15), jnp.bfloat16)]
        got["expand"] = contract_rows(jnp.concatenate(more, axis=1), d_pre).astype(jnp.bfloat16)
        return got["expand"]

    def hidden_work(half, done):
        tokens_all = after(tokens_line, done)
        got["hidden", half] = hidden_forward(tokens_all, shared, full_offsets[0], half)
        return got["hidden", half]

    def project_part(d_part, half):
        return lax.dot_general(
            d_part,
            got["hidden", half],
            (((1,), (0,)), ((), ())),
            preferred_element_type=jnp.float32,
        )

    def theirs_work(half, *done):
        theirs = project_part(after(d_theirs, *done), half).astype(jnp.bfloat16)
        got["sent", half] = lax.ppermute(theirs, "spot", [(i, i ^ 1) for i in range(inner)])
        return theirs

    def mine_work(half, done):
        mine = project_part(after(d_mine, done), half)
        got["sum", half] = mine + got["sent", half].astype(jnp.float32)
        spot = lax.axis_index("spot") // 2
        halves = got["sum", half].reshape(inner // 4, 2, columns, -1)
        theirs = pick(halves, 1 - spot % 2, 1).astype(jnp.bfloat16)
        got["sent", half] = lax.ppermute(theirs, "spot", [(i, i ^ 2) for i in range(inner)])
        return theirs

    def finish_work(half, done):
        spot = lax.axis_index("spot") // 2
        total = got["sum", half].reshape(inner // 4, 2, columns, -1)
        theirs = after(got["sent", half], done)
        total = pick(total, spot % 2, 1) + theirs.astype(jnp.float32)
        step = 4
        while total.shape[0] > 1:
            spot = spot // 2
            halves = total.reshape(total.shape[0] // 2, 2, columns, -1)
            theirs = pick(halves, 1 - spot % 2, 1).astype(jnp.bfloat16)
            theirs = lax.ppermute(theirs, "spot", [(i, i ^ step) for i in range(inner)])
            total = pick(halves, spot % 2, 1) + theirs.astype(jnp.float32)
            step *= 2
        total = total[0].astype(jnp.bfloat16)
        got["total", half] = total
        got["sent", half] = swap_groups(total, group)
        return total

    def swap_work(half, done):
        total = got["total", half]
        other = after(got["sent", half], done)
        got["project", half] = total.astype(jnp.float32) + other.astype(jnp.float32)
        if group != 2:
            got["project", half] = over_groups(total, group)
        return got["project", half]

    def work_two(done):
        return hidden_work(0, done)

    def work_three(done):
        sent = mine_work(0, theirs_work(0, done))
        got["order"] = finish_work(0, hidden_work(1, sent))
        return got["order"]

    def work_four(done):
        return mine_work(1, theirs_work(1, done, got["order"]))

    at = lax.axis_index("line") * inner * columns
    other = jnp.concatenate(
        [
            lax.dynamic_slice_in_dim(piece, at, inner * columns, 1)
            for piece in (near, far)
        ]
    )
    other = jnp.roll(other.reshape(2, quarter // 2, -1), core, 0).reshape(quarter, -1)
    sides = jnp.stack([lax.dynamic_slice_in_dim(own, at, inner * columns, 1), other])
    column_sides = jnp.roll(sides, plane, 0).reshape(2 * quarter, -1)
    column_shared = lax.dynamic_slice(
        shared, (width, at), (depth // 2, inner * columns)
    )
    got["columns", 0] = column_shared
    got["columns", 1] = column_sides

    def readout_part(half, *done):
        return jnp.dot(
            after(got["hidden", half], *done),
            got["columns", half],
            preferred_element_type=jnp.float32,
        )

    def work_five(done):
        at = lax.axis_index("line") * inner * columns
        bias = lax.dynamic_slice_in_dim(full_offsets[1], at, inner * columns, 0)
        out = readout_part(0, done) + bias
        first = swap_work(0, out)
        second = finish_work(1, out)
        out = out + readout_part(1, first, second)
        got["out"] = out.astype(jnp.bfloat16)
        return got["out"]

    g_one = spread_reduce(g_one, [expand_work, work_two, work_three, work_four, work_five])
    swap_work(1, got["out"])
    g_expand = lax.psum_scatter(got["expand"], WIDE, scatter_dimension=1, tiled=True)
    g_expand = after(g_expand, got["out"])
    g_expand = jnp.concatenate(
        [g_expand[: width + 1], g_out[None].astype(jnp.bfloat16), g_expand[width + 2 :]]
    )
    g_expand = over_groups(g_expand, group)
    g_offsets = g_expand[width : width + 2]
    g_expand = g_expand[:width]
    g_project = jnp.concatenate([got["project", 0], got["project", 1]], axis=1)
    out_line = got["out"].reshape(LINE * part, inner, columns).transpose(1, 0, 2)
    out_cols = lax.all_to_all(out_line, "spot", split_axis=0, concat_axis=0, tiled=True)
    readout = (
        out_cols.reshape(inner, LINE, part, columns)
        .transpose(1, 0, 2, 3)
        .reshape(-1, POOL * POOL, columns)
    )
    g_filters = jnp.stack(
        [g_one[:share], g_one[share : 2 * share], g_two[:share], g_two[share : 2 * share]]
    ).astype(jnp.float32)
    g_vectors = jnp.stack(
        [g_one[2 * share, : 15 * lanes], g_two[2 * share, : 15 * lanes]]
    ).reshape(2, 15, lanes).astype(jnp.float32)
    filters_out = adamw(
        filters, g_filters, filters_moment, filters_square, filters_average, 0.03, 0.05
    )
    vectors_out = adamw(
        vectors, g_vectors, vectors_moment, vectors_square, vectors_average, 0.3, 0.0
    )
    expand_out = adamw(expand, g_expand, expand_moment, expand_square, expand_average, 0.03, 0.05)
    project_out = adamw_turned(
        project, g_project, project_moment, project_square, project_average, 0.016, 0.05
    )
    offsets_out = adamw(
        offsets, g_offsets, offsets_moment, offsets_square, offsets_average, 0.1, 0.0
    )
    return (
        readout,
        patch_gradient,
        filters_out[0],
        filters_out[1],
        filters_out[2],
        filters_out[3],
        filters_out[4],
        vectors_out[0],
        vectors_out[1],
        vectors_out[2],
        vectors_out[3],
        vectors_out[4],
        expand_out[0],
        expand_out[1],
        expand_out[2],
        expand_out[3],
        expand_out[4],
        project_out[0],
        project_out[1],
        project_out[2],
        project_out[3],
        project_out[4],
        offsets_out[0],
        offsets_out[1],
        offsets_out[2],
        offsets_out[3],
        offsets_out[4],
    )


def solution(mesh):
    in_specs = (
        P(ALL, None, None),
        P(ALL),
        P("dp", None, WIDE),
        P(None, ALL, None),
        P(None, ALL, None),
        P(None, ALL, None),
        P(None, ALL, None),
        P(None, None, ALL),
        P(None, None, ALL),
        P(None, None, ALL),
        P(None, None, ALL),
        P(None, WIDE),
        P(None, WIDE),
        P(None, WIDE),
        P(None, WIDE),
        P(None, WIDE),
        P(None, WIDE),
        P(None, WIDE),
        P(None, WIDE),
        P(None, WIDE),
        P(None, WIDE),
        P(None, WIDE),
        P(None, WIDE),
    )
    out_specs = (
        P("dp", None, WIDE),
        P(ALL, None, None),
        P(None, ALL, None),
        P(None, ALL, None),
        P(None, ALL, None),
        P(None, ALL, None),
        P(None, ALL, None),
        P(None, None, ALL),
        P(None, None, ALL),
        P(None, None, ALL),
        P(None, None, ALL),
        P(None, None, ALL),
        P(None, WIDE),
        P(None, WIDE),
        P(None, WIDE),
        P(None, WIDE),
        P(None, WIDE),
        P(None, WIDE),
        P(None, WIDE),
        P(None, WIDE),
        P(None, WIDE),
        P(None, WIDE),
        P(None, WIDE),
        P(None, WIDE),
        P(None, WIDE),
        P(None, WIDE),
        P(None, WIDE),
    )
    devices = mesh.devices
    lines = Mesh(
        devices.reshape(devices.shape[0], LINE, devices.shape[1] // LINE), ("dp", "line", "spot")
    )
    return jax.shard_map(shards, mesh=lines, in_specs=in_specs, out_specs=out_specs, check_vma=False)
```

```python
import math
from functools import partial

import jax
import jax.numpy as jnp
from jax import lax
from jax.experimental import pallas as pl
from jax.experimental.pallas import tpu as pltpu
from jax.sharding import Mesh
from jax.sharding import PartitionSpec as P

GRID = 24
POOL = 12
SLOTS = 4
STEP = 3
LINE = 4
WIDE = ("line", "spot")
ALL = ("dp", "line", "spot")


beta_one = 0.5
beta_two = 0.5
adam_eps = 1e-08
ema_keep = 0.75
norm_eps = 1e-06


def contract_rows(left, right):
    return lax.dot_general(
        left, right, (((0,), (0,)), ((), ())), preferred_element_type=jnp.float32
    )


def contract_cols(left, right):
    return lax.dot_general(
        left, right, (((1,), (1,)), ((), ())), preferred_element_type=jnp.float32
    )


CHUNK = 48
LANE = 128


def shape_of(shape, kind):
    return jax.ShapeDtypeStruct(shape, kind)


def sigmoid(value):
    return 0.5 * jnp.tanh(0.5 * value) + 0.5


def fold_rows(value):
    return jnp.sum(value.reshape(value.shape[0] // 8, 8, value.shape[1]), axis=0)


def row_span(k, size):
    return pl.ds(pl.multiple_of(k * size, 16), size)


def lane_span(j):
    return pl.ds(j * LANE, LANE)


def row_total(parts):
    total = parts[0]
    for part in parts[1:]:
        total = total + part
    return jnp.sum(total, axis=1, keepdims=True)


def normalize(read, norm_ref, scale_ref, span, finish):
    width = norm_ref.shape[1]
    spans = [lane_span(j) for j in range(width // LANE)]
    center = row_total([read(lanes) for lanes in spans]) * (1.0 / width)
    spread = row_total([jnp.square(read(lanes) - center) for lanes in spans]) * (1.0 / width)
    scale = lax.rsqrt(spread + norm_eps)
    scale_ref[span, :] = jnp.broadcast_to(scale, (span.size, LANE))
    for lanes in spans:
        unit = (read(lanes) - center) * scale
        norm_ref[span, lanes] = unit
        finish(lanes, unit)


def shift_rows(value, amount, mask):
    return pltpu.roll(value, amount % value.shape[0], 0) * mask


def masks_for(side, rows):
    cell = jnp.arange(rows, dtype=jnp.int32)
    x, y = cell % side, (cell // side) % side
    flags = jnp.stack([x > 0, x < side - 1, y > 0, y < side - 1]).astype(jnp.float32)
    return jnp.broadcast_to(flags[:, :, None], (4, rows, LANE))


def conv_block(above, level, below, taps, mask_ref):
    columns = [
        taps[c] * above + taps[3 + c] * level + taps[6 + c] * below for c in range(3)
    ]
    return (
        columns[1]
        + shift_rows(columns[0], 1, mask_ref[0])
        + shift_rows(columns[2], -1, mask_ref[1])
    )


def taps_at(vec_ref, lanes):
    return [vec_ref[k : k + 1, lanes] for k in range(9)]


def forward_kernel(side, *refs):
    pooled = side == GRID
    if pooled:
        x_ref, in_ref, out_ref, vec_ref, mask_ref, pool_ref = refs[:6]
        n1_ref, n2_ref, n3_ref, r1_ref, r2_ref, r3_ref, b_ref, y_ref = refs[6:14]
        lin_ref, act_ref, hi_ref, lo_ref = refs[14:]
    else:
        live_ref, x_ref, in_ref, out_ref, vec_ref, mask_ref = refs[:6]
        n1_ref, n2_ref, n3_ref, r1_ref, r2_ref, r3_ref, b_ref, y_ref = refs[6:14]
        lin_ref, act_ref = refs[14:]
    rows, width = x_ref.shape
    count = rows // CHUNK
    edge = side if pooled else 0
    lin_ref[...] = jnp.dot(x_ref[...], in_ref[...], preferred_element_type=jnp.float32)
    if pooled:
        act_ref[0:side, :] = jnp.zeros((side, width), jnp.float32)
        act_ref[rows + side : rows + 2 * side, :] = jnp.zeros((side, width), jnp.float32)

    @pl.loop(0, count)
    def _(k):
        span = row_span(k, CHUNK)
        above = pl.ds(pl.multiple_of(k * CHUNK + edge, 8), CHUNK)

        def finish(lanes, unit):
            value = unit * vec_ref[9:10, lanes] + vec_ref[10:11, lanes]
            act_ref[above, lanes] = value * sigmoid(value)

        normalize(lambda lanes: lin_ref[span, lanes], n1_ref, r1_ref, span, finish)

    if pooled:

        @pl.loop(0, count)
        def _(k):
            for j in range(width // LANE):
                lanes = lane_span(j)
                near = [
                    act_ref[pl.ds(pl.multiple_of(k * CHUNK + r * side, 8), CHUNK), lanes]
                    for r in range(3)
                ]
                lin_ref[row_span(k, CHUNK), lanes] = conv_block(
                    near[0], near[1], near[2], taps_at(vec_ref, lanes), mask_ref
                )
    else:
        cells = side * side

        @pl.loop(0, rows // cells)
        def _(k):
            for j in range(width // LANE):
                lanes = lane_span(j)
                level = act_ref[row_span(k, cells), lanes]
                lin_ref[row_span(k, cells), lanes] = conv_block(
                    shift_rows(level, side, mask_ref[2]),
                    level,
                    shift_rows(level, -side, mask_ref[3]),
                    taps_at(vec_ref, lanes),
                    mask_ref,
                )

    @pl.loop(0, count)
    def _(k):
        span = row_span(k, CHUNK)

        def finish(lanes, unit):
            value = unit * vec_ref[11:12, lanes] + vec_ref[12:13, lanes]
            b_ref[span, lanes] = (value * sigmoid(value)).astype(jnp.bfloat16)

        normalize(lambda lanes: lin_ref[span, lanes], n2_ref, r2_ref, span, finish)

    lin_ref[...] = jnp.dot(b_ref[...], out_ref[...], preferred_element_type=jnp.float32)

    @pl.loop(0, count)
    def _(k):
        span = row_span(k, CHUNK)
        if not pooled:
            scale = live_ref[k * CHUNK // (side * side)]

        def finish(lanes, unit):
            value = (
                x_ref[span, lanes].astype(jnp.float32)
                + unit * vec_ref[13:14, lanes]
                + vec_ref[14:15, lanes]
            )
            value = value * sigmoid(value)
            if pooled:
                high = value.astype(jnp.bfloat16)
                hi_ref[span, lanes] = high
                lo_ref[span, lanes] = (value - high.astype(jnp.float32)).astype(jnp.bfloat16)
            else:
                y_ref[span, lanes] = (value * scale).astype(jnp.bfloat16)

        normalize(lambda lanes: lin_ref[span, lanes], n3_ref, r3_ref, span, finish)

    if pooled:
        y_ref[...] = (
            jnp.dot(pool_ref[...], hi_ref[...], preferred_element_type=jnp.float32)
            + jnp.dot(pool_ref[...], lo_ref[...], preferred_element_type=jnp.float32)
        ).astype(jnp.bfloat16)


def backward_kernel(side, *refs):
    pooled = side == GRID
    if pooled:
        up_ref, d_ref, x_ref, in_ref, out_ref, vec_ref, mask_ref = refs[:7]
    else:
        live_ref, d_ref, x_ref, in_ref, out_ref, vec_ref, mask_ref = refs[:7]
    n1_ref, n2_ref, n3_ref, r1_ref, r2_ref, r3_ref = refs[7:13]
    dx_ref, da_ref, dc_ref, sum_ref = refs[13:17]
    res_ref, mix_ref, act_ref = refs[17:20]
    rows, width = x_ref.shape
    count = rows // CHUNK
    edge = side if pooled else 0
    spans = [lane_span(j) for j in range(width // LANE)]

    @pl.when(pl.program_id(0) == 0)
    def _():
        sum_ref[...] = jnp.zeros(sum_ref.shape, jnp.float32)

    def add_sum(k, lanes, value):
        sum_ref[8 * k : 8 * k + 8, lanes] += fold_rows(value)

    if pooled:
        grads = d_ref[...]
        high = grads.astype(jnp.bfloat16)
        low = (grads - high.astype(jnp.float32)).astype(jnp.bfloat16)
        res_ref[...] = jnp.dot(
            up_ref[...], high, preferred_element_type=jnp.float32
        ) + jnp.dot(up_ref[...], low, preferred_element_type=jnp.float32)

    def norm_back(unit_ref, scale_ref, span, gain, read_grad, store):
        first, second = [], []
        for lanes in spans:
            grad = read_grad(lanes) * vec_ref[gain : gain + 1, lanes]
            first.append(grad)
            second.append(grad * unit_ref[span, lanes])
        mean_grad = row_total(first) * (1.0 / width)
        mean_unit = row_total(second) * (1.0 / width)
        for lanes in spans:
            grad = read_grad(lanes) * vec_ref[gain : gain + 1, lanes]
            store(
                lanes,
                scale_ref[span, :]
                * (grad - mean_grad - unit_ref[span, lanes] * mean_unit),
            )

    @pl.loop(0, count)
    def _(k):
        span = row_span(k, CHUNK)
        if not pooled:
            scale = live_ref[k * CHUNK // (side * side)]
        for lanes in spans:
            unit = n3_ref[span, lanes]
            value = (
                x_ref[span, lanes].astype(jnp.float32)
                + unit * vec_ref[13:14, lanes]
                + vec_ref[14:15, lanes]
            )
            gate = sigmoid(value)
            grad = res_ref[span, lanes] if pooled else d_ref[span, lanes] * scale
            grad = grad * (gate * (1.0 + value * (1.0 - gate)))
            res_ref[span, lanes] = grad
            add_sum(13, lanes, grad * unit)
            add_sum(14, lanes, grad)

        def store(lanes, value):
            dc_ref[span, lanes] = value.astype(jnp.bfloat16)

        norm_back(n3_ref, r3_ref, span, 13, lambda lanes: res_ref[span, lanes], store)

    if pooled:
        mix_ref[0:side, :] = jnp.zeros((side, width), jnp.float32)
        mix_ref[rows + side : rows + 2 * side, :] = jnp.zeros((side, width), jnp.float32)
    mix_ref[edge : rows + edge, :] = contract_cols(dc_ref[...], out_ref[...])

    @pl.loop(0, count)
    def _(k):
        span = row_span(k, CHUNK)
        at = pl.ds(pl.multiple_of(k * CHUNK + edge, 8), CHUNK)
        for lanes in spans:
            unit = n2_ref[span, lanes]
            value = unit * vec_ref[11:12, lanes] + vec_ref[12:13, lanes]
            gate = sigmoid(value)
            grad = mix_ref[at, lanes] * (gate * (1.0 + value * (1.0 - gate)))
            mix_ref[at, lanes] = grad
            add_sum(11, lanes, grad * unit)
            add_sum(12, lanes, grad)

        def store(lanes, value):
            mix_ref[at, lanes] = value

        norm_back(n2_ref, r2_ref, span, 11, lambda lanes: mix_ref[at, lanes], store)

    size = CHUNK if pooled else side * side

    @pl.loop(0, rows // size)
    def _(k):
        span = row_span(k, size)
        for lanes in spans:
            if pooled:
                near = [
                    mix_ref[pl.ds(pl.multiple_of(k * size + (2 - r) * side, 8), size), lanes]
                    for r in range(3)
                ]
            else:
                level = mix_ref[span, lanes]
                near = [
                    shift_rows(level, -side, mask_ref[3]),
                    level,
                    shift_rows(level, side, mask_ref[2]),
                ]
            taps = taps_at(vec_ref, lanes)
            mixed = [
                taps[c] * near[0] + taps[3 + c] * near[1] + taps[6 + c] * near[2]
                for c in range(3)
            ]
            grad = (
                mixed[1]
                + shift_rows(mixed[0], -1, mask_ref[1])
                + shift_rows(mixed[2], 1, mask_ref[0])
            )
            unit = n1_ref[span, lanes]
            value = unit * vec_ref[9:10, lanes] + vec_ref[10:11, lanes]
            gate = sigmoid(value)
            active = value * gate
            sides = [
                shift_rows(active, 1, mask_ref[0]),
                active,
                shift_rows(active, -1, mask_ref[1]),
            ]
            for r in range(3):
                for c in range(3):
                    add_sum(3 * r + c, lanes, sides[c] * near[r])
            grad = grad * (gate * (1.0 + value * (1.0 - gate)))
            act_ref[span, lanes] = grad
            add_sum(9, lanes, grad * unit)
            add_sum(10, lanes, grad)

    @pl.loop(0, count)
    def _(k):
        span = row_span(k, CHUNK)

        def store(lanes, value):
            da_ref[span, lanes] = value.astype(jnp.bfloat16)

        norm_back(n1_ref, r1_ref, span, 9, lambda lanes: act_ref[span, lanes], store)

    step = 256
    for j in range(width // step):
        dx_ref[:, j * step : (j + 1) * step] = (
            res_ref[:, j * step : (j + 1) * step]
            + contract_cols(da_ref[...], in_ref[j * step : (j + 1) * step, :])
        ).astype(dx_ref.dtype)


def pool_matrix():
    cell = jnp.arange(GRID * GRID, dtype=jnp.int32)
    home = (cell // GRID // 2) * POOL + (cell % GRID) // 2
    spot = jnp.arange(POOL * POOL, dtype=jnp.int32)
    return jnp.where(home[None, :] == spot[:, None], 0.25, 0.0).astype(jnp.bfloat16)


def block_specs(side, rows, width):
    whole = lambda shape: pl.BlockSpec(shape, lambda i: (0,) * len(shape))
    part = lambda cells, lanes: pl.BlockSpec((cells, lanes), lambda i: (i, 0))
    size = side * side if side == GRID else rows
    return whole, part, size


def kernel_params(axes=1):
    return pltpu.CompilerParams(
        dimension_semantics=("arbitrary",) * axes, vmem_limit_bytes=60 * 1024 * 1024
    )


def block_forward(rows, w_in, w_out, vecs, side, live=None):
    total, width = rows.shape
    whole, part, size = block_specs(side, total, width)
    pooled = side == GRID
    mask_rows = CHUNK if pooled else side * side
    vecs = jnp.pad(vecs, ((0, 1), (0, 0)))
    masks = masks_for(side, mask_rows)
    norm = shape_of((total, width), jnp.float32)
    scale = shape_of((total, LANE), jnp.float32)
    out_cells = POOL * POOL if pooled else size
    operands = [rows, w_in, w_out, vecs, masks]
    in_specs = [
        part(size, width),
        whole(w_in.shape),
        whole(w_out.shape),
        whole(vecs.shape),
        whole(masks.shape),
    ]
    scratch = [
        pltpu.VMEM((size, width), jnp.float32),
        pltpu.VMEM((size + 2 * side, width) if pooled else (size, width), jnp.float32),
    ]
    if pooled:
        operands.append(pool_matrix())
        in_specs.append(whole((POOL * POOL, GRID * GRID)))
        scratch += [pltpu.VMEM((size, width), jnp.bfloat16)] * 2
    else:
        operands.insert(0, live)
        in_specs.insert(0, pl.BlockSpec(memory_space=pltpu.SMEM))
    outs = pl.pallas_call(
        partial(forward_kernel, side),
        grid=(total // size,),
        in_specs=in_specs,
        out_specs=[part(size, width)] * 3
        + [part(size, LANE)] * 3
        + [part(size, width), part(out_cells, width)],
        out_shape=[norm] * 3
        + [scale] * 3
        + [
            shape_of((total, width), jnp.bfloat16),
            shape_of((total // size * out_cells, width), jnp.bfloat16),
        ],
        scratch_shapes=scratch,
        compiler_params=kernel_params(),
        name="block_forward_" + str(side),
    )(*operands)
    return outs[7], (rows, outs[6], tuple(outs[:6]))


def block_backward(d_result, saved, w_in, w_out, vecs, side, live=None):
    rows, narrow, kept = saved
    total, width = rows.shape
    whole, part, size = block_specs(side, total, width)
    pooled = side == GRID
    mask_rows = CHUNK if pooled else side * side
    vecs = jnp.pad(vecs, ((0, 1), (0, 0)))
    masks = masks_for(side, mask_rows)
    in_cells = POOL * POOL if pooled else size
    if pooled:
        first = pool_matrix().T
        first_spec = whole(first.shape)
    else:
        first = live
        first_spec = pl.BlockSpec(memory_space=pltpu.SMEM)
    low = shape_of((total, width), jnp.bfloat16)
    dx, da, dc, sums = pl.pallas_call(
        partial(backward_kernel, side),
        grid=(total // size,),
        in_specs=[
            first_spec,
            part(in_cells, width),
            part(size, width),
            whole(w_in.shape),
            whole(w_out.shape),
            whole(vecs.shape),
            whole(masks.shape),
        ]
        + [part(size, width)] * 3
        + [part(size, LANE)] * 3,
        out_specs=[part(size, width)] * 3 + [whole((128, width))],
        out_shape=[
            shape_of((total, width), jnp.bfloat16 if pooled else jnp.float32),
            low,
            low,
            shape_of((128, width), jnp.float32),
        ],
        scratch_shapes=[
            pltpu.VMEM((size, width), jnp.float32),
            pltpu.VMEM((size + 2 * side, width) if pooled else (size, width), jnp.float32),
            pltpu.VMEM((size, width), jnp.float32),
        ],
        compiler_params=kernel_params(),
        name="block_backward_" + str(side),
    )(first, d_result, rows, w_in, w_out, vecs, masks, *kept)
    grad_out = contract_rows(narrow, dc)
    grad_in = contract_rows(rows, da)
    grad_vecs = jnp.sum(sums[:120].reshape(15, 8, width), axis=1)
    return dx, grad_in, grad_out, grad_vecs


def adamw(weight, grad, moment, square, average, rate, decay):
    momentum = beta_one * moment + (1.0 - beta_one) * grad
    variance = beta_two * square + (1.0 - beta_two) * grad * grad
    scaled_m = momentum / (1.0 - beta_one**STEP)
    scaled_v = variance / (1.0 - beta_two**STEP)
    updated = weight - rate * (scaled_m / (jnp.sqrt(scaled_v) + adam_eps) + decay * weight)
    smoothed = ema_keep * average + (1.0 - ema_keep) * updated
    return (updated, momentum, variance, smoothed, updated.astype(jnp.bfloat16))


def pad_row(row, width):
    return jnp.pad(row, ((0, 0), (0, width - row.shape[1])))


def ring_order(chips):
    inner = chips // LINE
    cells = [(o, 0) for o in range(LINE)]
    for turn, o in enumerate(reversed(range(LINE))):
        line = list(range(1, inner))
        cells += [(o, i) for i in (line if turn % 2 == 0 else line[::-1])]
    return [o * inner + i for o, i in cells]


def ring_gather(value, inner, group):
    chips = LINE * inner // 2
    ring = ring_order(chips)
    back = sorted(range(chips), key=lambda place: ring[place])
    index = lax.axis_index(WIDE)
    core = index % 2
    place = jnp.asarray(back, jnp.int32)[index // 2]
    turn = 1 - 2 * core
    pairs = []
    for r in range(chips):
        ahead, behind = ring[(r + 1) % chips], ring[(r - 1) % chips]
        pairs += [(ring[r] * 2, ahead * 2), (ring[r] * 2 + 1, behind * 2 + 1)]
    spots = jnp.asarray(ring, jnp.int32)
    held_all = jnp.zeros((chips,) + value.shape, value.dtype)
    for s in range(chips):
        if s:
            value = lax.ppermute(value, WIDE, pairs)
        if s == chips // 2:
            middle = value
        spot = spots[(place - turn * s) % chips]
        held_all = lax.dynamic_update_index_in_dim(held_all, value, spot, 0)
    if group == 2:
        other = lax.ppermute(held_all, "dp", [(0, 1), (1, 0)])
        first = lax.axis_index("dp") == 0
        planes = jnp.stack(
            [jnp.where(first, held_all, other), jnp.where(first, other, held_all)]
        )
    else:
        planes = lax.all_gather(held_all, "dp", axis=0)
    other = lax.ppermute(planes, "spot", [(i, i ^ 1) for i in range(inner)])
    first = core == 0
    planes = jnp.stack([jnp.where(first, planes, other), jnp.where(first, other, planes)], axis=2)
    return planes, middle


def swap_groups(value, group):
    return lax.ppermute(value, "dp", [(i, i ^ 1) for i in range(group)])


def over_groups(value, group):
    if group == 2:
        other = lax.ppermute(value, "dp", [(0, 1), (1, 0)])
        return value.astype(jnp.float32) + other.astype(jnp.float32)
    return lax.psum(value, "dp").astype(jnp.float32)


def reduce_block(grad_in, grad_out, grad_vecs, devices):
    width = grad_in.shape[1]
    share = width // devices
    rows = [
        grad_in.astype(jnp.bfloat16).reshape(devices, share, width),
        grad_out.astype(jnp.bfloat16).reshape(devices, share, width),
        jnp.pad(
            grad_vecs.astype(jnp.bfloat16)
            .reshape(15, devices, share)
            .transpose(1, 0, 2)
            .reshape(devices, 1, 15 * share),
            ((0, 0), (0, 15), (0, width - 15 * share)),
        ),
    ]
    return jnp.concatenate(rows, axis=1)


def pick(value, at, axis):
    return lax.dynamic_index_in_dim(value, at, axis, False)


def after(value, *others):
    return lax.optimization_barrier((value,) + others)[0]


def spread_reduce(blocks, works):
    count = blocks.shape[0]
    bits = count.bit_length() - 1
    order = [0, 1] + list(range(bits - 1, 1, -1))
    me = lax.axis_index(ALL)
    blocks = blocks.reshape((2,) * bits + blocks.shape[1:])
    left = list(range(bits))[::-1]
    for stage, bit in enumerate(order):
        axis = left.index(bit)
        left.pop(axis)
        mine = (me >> bit) & 1
        pairs = [(i, i ^ (1 << bit)) for i in range(count)]
        sent = pick(blocks, 1 - mine, axis)
        theirs = lax.ppermute(sent, ALL, pairs)
        if stage < len(works):
            theirs = after(theirs, works[stage](blocks))
        blocks = (
            pick(blocks, mine, axis).astype(jnp.float32) + theirs.astype(jnp.float32)
        ).astype(jnp.bfloat16)
    return blocks


def held(value):
    return lax.optimization_barrier(value)


def gelu_slope(value):
    return 0.5 * (1.0 + lax.erf(value * (0.5**0.5))) + value * jnp.exp(-0.5 * value * value) * (
        0.5 / math.pi
    ) ** 0.5


def hidden_kernel(tokens_ref, expand_ref, bias_ref, out_ref):
    pre = jnp.dot(tokens_ref[...], expand_ref[...], preferred_element_type=jnp.float32)
    pre = pre + bias_ref[...]
    out_ref[...] = (0.5 * pre * (1.0 + lax.erf(pre * (0.5**0.5)))).astype(jnp.bfloat16)


def hidden_forward(tokens, readers, bias, half):
    total, width = tokens.shape
    depth = readers.shape[1] // 2
    rows, step = total // LINE, 512
    skip = half * depth // step
    return pl.pallas_call(
        hidden_kernel,
        grid=(depth // step, LINE),
        in_specs=[
            pl.BlockSpec((rows, width), lambda j, i: (i, 0)),
            pl.BlockSpec((width, step), lambda j, i: (0, j + skip)),
            pl.BlockSpec((1, step), lambda j, i: (0, j + skip)),
        ],
        out_specs=pl.BlockSpec((rows, step), lambda j, i: (i, j)),
        out_shape=shape_of((total, depth), jnp.bfloat16),
        compiler_params=kernel_params(2),
        name="hidden_forward",
    )(tokens, readers, bias[None])


def adamw_kernel(rate, decay, grad_ref, *refs):
    old, new = refs[:4], refs[4:]
    results = adamw(old[0][...], grad_ref[...].T, *[ref[...] for ref in old[1:]], rate, decay)
    for ref, result in zip(new, results):
        ref[...] = result


def adamw_turned(weight, grad, moment, square, average, rate, decay):
    depth, columns = weight.shape
    step = 512
    part = pl.BlockSpec((step, columns), lambda i: (i, 0))
    return pl.pallas_call(
        partial(adamw_kernel, rate, decay),
        grid=(depth // step,),
        in_specs=[pl.BlockSpec((columns, step), lambda i: (0, i))] + [part] * 4,
        out_specs=[part] * 5,
        out_shape=[shape_of(weight.shape, jnp.float32)] * 4
        + [shape_of(weight.shape, jnp.bfloat16)],
        compiler_params=kernel_params(),
        name="adamw_turned",
    )(grad, weight, moment, square, average)


def pre_kernel(counts, at_ref, d_ref, tokens_ref, *refs):
    sources, (expand_ref, bias_ref, out_ref) = refs[: len(counts)], refs[len(counts) :]
    pre = jnp.dot(tokens_ref[...], expand_ref[...], preferred_element_type=jnp.float32)
    slope = gelu_slope(pre + bias_ref[...])
    index = pl.program_id(0)
    start = 0
    for count, source in zip(counts, sources):

        @pl.when((index >= start) & (index < start + count))
        def _(source=source):
            grad = contract_cols(d_ref[...], source[...])
            out_ref[...] = (grad * slope).astype(jnp.bfloat16)

        start += count


def pre_backward(d_full, tokens, shared, bias, pieces):
    rows, width = tokens.shape
    depth = d_full.shape[1]
    step = 512
    counts = [size // step for _, _, _, size in pieces]
    order = jnp.concatenate(
        [
            jnp.asarray(start // step, jnp.int32) + jnp.arange(size // step, dtype=jnp.int32)
            for _, _, start, size in pieces
        ]
    )
    specs = []
    first = 0
    for (source, skip, _, size), count in zip(pieces, counts):
        low, high = skip // step, skip // step + count - 1
        specs.append(
            pl.BlockSpec(
                (step, depth),
                lambda i, at, low=low, high=high, first=first: (
                    jnp.clip(i - first + low, low, high),
                    0,
                ),
            )
        )
        first += count
    return pl.pallas_call(
        partial(pre_kernel, counts),
        grid_spec=pltpu.PrefetchScalarGridSpec(
            num_scalar_prefetch=1,
            grid=(depth // step,),
            in_specs=[
                pl.BlockSpec((rows, depth), lambda i, at: (0, 0)),
                pl.BlockSpec((rows, width), lambda i, at: (0, 0)),
            ]
            + specs
            + [
                pl.BlockSpec((width, step), lambda i, at: (0, at[i])),
                pl.BlockSpec((1, step), lambda i, at: (0, at[i])),
            ],
            out_specs=pl.BlockSpec((rows, step), lambda i, at: (0, at[i])),
        ),
        out_shape=shape_of((rows, depth), jnp.bfloat16),
        compiler_params=kernel_params(),
        name="pre_backward",
    )(order, d_full, tokens, *[piece[0] for piece in pieces], shared, bias[None])


def shards(
    patches,
    counts,
    cotangent,
    filters,
    filters_moment,
    filters_square,
    filters_average,
    vectors,
    vectors_moment,
    vectors_square,
    vectors_average,
    expand,
    expand_moment,
    expand_square,
    expand_average,
    project,
    project_moment,
    project_square,
    project_average,
    offsets,
    offsets_moment,
    offsets_square,
    offsets_average,
):
    inner = lax.axis_size("spot")
    wide = LINE * inner
    group = lax.axis_size("dp")
    devices = wide * group
    share = filters.shape[1]
    lanes = vectors.shape[2]
    columns = expand.shape[1]
    packed = jnp.concatenate(
        [
            filters.astype(jnp.bfloat16).reshape(4 * share, filters.shape[2]),
            pad_row(vectors.astype(jnp.bfloat16).reshape(1, -1), filters.shape[2]),
            pad_row(offsets.astype(jnp.bfloat16).reshape(1, -1), filters.shape[2]),
            jnp.zeros((14, filters.shape[2]), jnp.bfloat16),
        ]
    )
    spread, middle = ring_gather(packed, inner, group)
    whole_filters = [
        spread[:, :, :, k * share : (k + 1) * share].reshape(devices * share, -1)
        for k in range(4)
    ]
    spread = spread[:, :, :, 4 * share : 4 * share + 2].reshape(devices, 2, -1)
    vec_full = (
        spread[:, 0, : 30 * lanes]
        .reshape(devices, 2, 15, lanes)
        .transpose(1, 2, 0, 3)
        .reshape(2, 15, devices * lanes)
        .astype(jnp.float32)
    )
    full_offsets = (
        spread[:wide, 1, : 2 * columns]
        .reshape(wide, 2, columns)
        .transpose(1, 0, 2)
        .reshape(2, wide * columns)
        .astype(jnp.float32)
    )
    images = patches.shape[0]
    width = patches.shape[2]
    samples = counts.shape[0]
    image_index = jnp.arange(images, dtype=jnp.int32)
    owner = image_index // SLOTS
    slot = image_index % SLOTS
    matches = owner[:, None] == jnp.arange(samples, dtype=jnp.int32)[None, :]
    chosen = jnp.sum(jnp.where(matches, counts[None, :], 0), axis=1)
    live = (slot < chosen).astype(jnp.float32)
    rows = patches.reshape(images * GRID * GRID, width)
    d_cols = cotangent.reshape(-1, columns)
    part = d_cols.shape[0] // wide
    plane = lax.axis_index("dp") % 2
    swap = [(i, i ^ 1) for i in range(inner)]
    cross = [(i, i ^ 1) for i in range(group)]
    core = lax.axis_index("spot") % 2
    depth = project.shape[0]
    quarter = depth // 4
    project_low = project.astype(jnp.bfloat16)
    own = lax.dynamic_slice_in_dim(project_low, depth // 2 + plane * quarter, quarter, 0)
    shared = jnp.concatenate([expand.astype(jnp.bfloat16), project_low[: depth // 2]])
    own = lax.all_gather(own, WIDE, axis=1, tiled=True)
    shared = lax.all_gather(after(shared, middle), WIDE, axis=1, tiled=True)
    near = pick(after(own, whole_filters[0]).reshape(2, quarter // 2, -1), core, 0)
    near = lax.ppermute(near, "dp", cross)
    pooled, first_saved = block_forward(
        rows, whole_filters[0], whole_filters[1], vec_full[0], GRID
    )
    tokens, second_saved = block_forward(
        pooled, whole_filters[2], whole_filters[3], vec_full[1], POOL, live
    )
    near = after(near, tokens)
    far = lax.ppermute(near, "spot", swap)
    d_full = lax.all_to_all(d_cols, WIDE, split_axis=0, concat_axis=0, tiled=True)
    d_full = after(d_full, whole_filters[0]).reshape(wide, part, columns)
    d_full = d_full.transpose(1, 0, 2).reshape(part, wide * columns)
    g_out = jnp.sum(d_cols.astype(jnp.float32), axis=0)
    d_line = d_cols.reshape(LINE, inner, part, columns).transpose(1, 0, 2, 3)
    tokens_after, shared, d_line, d_full, g_out = lax.optimization_barrier(
        (tokens, shared, d_line, d_full, g_out)
    )
    full_expand = shared[:width]
    tokens_line = lax.all_gather(tokens_after, "line", axis=0, tiled=True)
    d_line = lax.all_to_all(d_line, "spot", split_axis=0, concat_axis=0, tiled=True)
    d_line = d_line.reshape(inner, LINE * part, columns)
    d_cores = d_line.reshape(inner // 2, 2, LINE * part, columns)
    near_at = depth // 2 + (1 - plane) * quarter + core * (quarter // 2)
    far_at = depth // 2 + (1 - plane) * quarter + (1 - core) * (quarter // 2)
    d_pre = pre_backward(
        d_full,
        tokens,
        shared,
        full_offsets[0],
        [
            (shared, width, 0, depth // 2),
            (own, 0, depth // 2 + plane * quarter, quarter),
            (near, 0, near_at, quarter // 2),
            (far, 0, far_at, quarter // 2),
        ],
    )
    d_tokens = contract_cols(d_pre, full_expand)
    d_pooled, g_in_two, g_out_two, g_vec_two = block_backward(
        d_tokens, second_saved, whole_filters[2], whole_filters[3], vec_full[1], POOL, live
    )
    g_two = reduce_block(g_in_two, g_out_two, g_vec_two, devices)
    d_pooled, g_two, d_theirs, d_mine = held(
        (d_pooled, g_two, pick(d_cores, 1 - core, 1), pick(d_cores, core, 1))
    )
    g_two = lax.psum_scatter(g_two, ALL, scatter_dimension=0, tiled=False)
    d_rows, g_in_one, g_out_one, g_vec_one = block_backward(
        d_pooled, first_saved, whole_filters[0], whole_filters[1], vec_full[0], GRID
    )
    patch_gradient = d_rows.reshape(images, GRID * GRID, width)
    g_one = reduce_block(g_in_one, g_out_one, g_vec_one, devices)
    got = {}

    def expand_work(done):
        ones = jnp.ones((tokens.shape[0], 1), jnp.bfloat16)
        more = [after(tokens, done), ones, jnp.zeros((tokens.shape[0], 15), jnp.bfloat16)]
        got["expand"] = contract_rows(jnp.concatenate(more, axis=1), d_pre).astype(jnp.bfloat16)
        return got["expand"]

    def hidden_work(half, done):
        tokens_all = after(tokens_line, done)
        got["hidden", half] = hidden_forward(tokens_all, shared, full_offsets[0], half)
        return got["hidden", half]

    def project_part(d_part, half):
        return lax.dot_general(
            d_part,
            got["hidden", half],
            (((1,), (0,)), ((), ())),
            preferred_element_type=jnp.float32,
        )

    def theirs_work(half, *done):
        theirs = project_part(after(d_theirs, *done), half).astype(jnp.bfloat16)
        got["sent", half] = lax.ppermute(theirs, "spot", [(i, i ^ 1) for i in range(inner)])
        return theirs

    def mine_work(half, done):
        d_part = after(d_mine, done)
        if half == 0:
            d_part, got["two"] = held((d_part, g_two))
        mine = project_part(d_part, half)
        got["sum", half] = mine + got["sent", half].astype(jnp.float32)
        spot = lax.axis_index("spot") // 2
        halves = got["sum", half].reshape(inner // 4, 2, columns, -1)
        theirs = pick(halves, 1 - spot % 2, 1).astype(jnp.bfloat16)
        got["sent", half] = lax.ppermute(theirs, "spot", [(i, i ^ 2) for i in range(inner)])
        return theirs

    def finish_work(half, done):
        spot = lax.axis_index("spot") // 2
        total = got["sum", half].reshape(inner // 4, 2, columns, -1)
        theirs = after(got["sent", half], done)
        total = pick(total, spot % 2, 1) + theirs.astype(jnp.float32)
        step = 4
        while total.shape[0] > 1:
            spot = spot // 2
            halves = total.reshape(total.shape[0] // 2, 2, columns, -1)
            theirs = pick(halves, 1 - spot % 2, 1).astype(jnp.bfloat16)
            theirs = lax.ppermute(theirs, "spot", [(i, i ^ step) for i in range(inner)])
            total = pick(halves, spot % 2, 1) + theirs.astype(jnp.float32)
            step *= 2
        total = total[0].astype(jnp.bfloat16)
        got["total", half] = total
        got["sent", half] = swap_groups(total, group)
        return total

    def swap_work(half, done):
        total = got["total", half]
        other = after(got["sent", half], done)
        got["project", half] = total.astype(jnp.float32) + other.astype(jnp.float32)
        if group != 2:
            got["project", half] = over_groups(total, group)
        return got["project", half]

    def work_two(done):
        return hidden_work(0, done)

    def work_three(done):
        sent = mine_work(0, theirs_work(0, done))
        got["order"] = finish_work(0, hidden_work(1, sent))
        return got["order"]

    def work_four(done):
        return mine_work(1, theirs_work(1, done, got["order"]))

    at = lax.axis_index("line") * inner * columns
    other = jnp.concatenate(
        [
            lax.dynamic_slice_in_dim(piece, at, inner * columns, 1)
            for piece in (near, far)
        ]
    )
    other = jnp.roll(other.reshape(2, quarter // 2, -1), core, 0).reshape(quarter, -1)
    sides = jnp.stack([lax.dynamic_slice_in_dim(own, at, inner * columns, 1), other])
    column_sides = jnp.roll(sides, plane, 0).reshape(2 * quarter, -1)
    column_shared = lax.dynamic_slice(
        shared, (width, at), (depth // 2, inner * columns)
    )
    got["columns", 0] = column_shared
    got["columns", 1] = column_sides

    def readout_part(half, *done):
        return jnp.dot(
            after(got["hidden", half], *done),
            got["columns", half],
            preferred_element_type=jnp.float32,
        )

    def work_five(done):
        at = lax.axis_index("line") * inner * columns
        bias = lax.dynamic_slice_in_dim(full_offsets[1], at, inner * columns, 0)
        out = readout_part(0, done) + bias
        first = swap_work(0, out)
        second = finish_work(1, out)
        out = out + readout_part(1, first, second)
        got["out"] = out.astype(jnp.bfloat16)
        return got["out"]

    g_one = spread_reduce(g_one, [expand_work, work_two, work_three, work_four, work_five])
    swap_work(1, got["out"])
    g_expand = lax.psum_scatter(got["expand"], WIDE, scatter_dimension=1, tiled=True)
    g_expand = after(g_expand, got["out"])
    g_expand = jnp.concatenate(
        [g_expand[: width + 1], g_out[None].astype(jnp.bfloat16), g_expand[width + 2 :]]
    )
    g_expand = over_groups(g_expand, group)
    g_offsets = g_expand[width : width + 2]
    g_expand = g_expand[:width]
    g_project = jnp.concatenate([got["project", 0], got["project", 1]], axis=1)
    out_line = got["out"].reshape(LINE * part, inner, columns).transpose(1, 0, 2)
    out_cols = lax.all_to_all(out_line, "spot", split_axis=0, concat_axis=0, tiled=True)
    readout = (
        out_cols.reshape(inner, LINE, part, columns)
        .transpose(1, 0, 2, 3)
        .reshape(-1, POOL * POOL, columns)
    )
    g_two = got["two"]
    g_filters = jnp.stack(
        [g_one[:share], g_one[share : 2 * share], g_two[:share], g_two[share : 2 * share]]
    ).astype(jnp.float32)
    g_vectors = jnp.stack(
        [g_one[2 * share, : 15 * lanes], g_two[2 * share, : 15 * lanes]]
    ).reshape(2, 15, lanes).astype(jnp.float32)
    filters_out = adamw(
        filters, g_filters, filters_moment, filters_square, filters_average, 0.03, 0.05
    )
    vectors_out = adamw(
        vectors, g_vectors, vectors_moment, vectors_square, vectors_average, 0.3, 0.0
    )
    expand_out = adamw(expand, g_expand, expand_moment, expand_square, expand_average, 0.03, 0.05)
    project_out = adamw_turned(
        project, g_project, project_moment, project_square, project_average, 0.016, 0.05
    )
    offsets_out = adamw(
        offsets, g_offsets, offsets_moment, offsets_square, offsets_average, 0.1, 0.0
    )
    return (
        readout,
        patch_gradient,
        filters_out[0],
        filters_out[1],
        filters_out[2],
        filters_out[3],
        filters_out[4],
        vectors_out[0],
        vectors_out[1],
        vectors_out[2],
        vectors_out[3],
        vectors_out[4],
        expand_out[0],
        expand_out[1],
        expand_out[2],
        expand_out[3],
        expand_out[4],
        project_out[0],
        project_out[1],
        project_out[2],
        project_out[3],
        project_out[4],
        offsets_out[0],
        offsets_out[1],
        offsets_out[2],
        offsets_out[3],
        offsets_out[4],
    )


def solution(mesh):
    in_specs = (
        P(ALL, None, None),
        P(ALL),
        P("dp", None, WIDE),
        P(None, ALL, None),
        P(None, ALL, None),
        P(None, ALL, None),
        P(None, ALL, None),
        P(None, None, ALL),
        P(None, None, ALL),
        P(None, None, ALL),
        P(None, None, ALL),
        P(None, WIDE),
        P(None, WIDE),
        P(None, WIDE),
        P(None, WIDE),
        P(None, WIDE),
        P(None, WIDE),
        P(None, WIDE),
        P(None, WIDE),
        P(None, WIDE),
        P(None, WIDE),
        P(None, WIDE),
        P(None, WIDE),
    )
    out_specs = (
        P("dp", None, WIDE),
        P(ALL, None, None),
        P(None, ALL, None),
        P(None, ALL, None),
        P(None, ALL, None),
        P(None, ALL, None),
        P(None, ALL, None),
        P(None, None, ALL),
        P(None, None, ALL),
        P(None, None, ALL),
        P(None, None, ALL),
        P(None, None, ALL),
        P(None, WIDE),
        P(None, WIDE),
        P(None, WIDE),
        P(None, WIDE),
        P(None, WIDE),
        P(None, WIDE),
        P(None, WIDE),
        P(None, WIDE),
        P(None, WIDE),
        P(None, WIDE),
        P(None, WIDE),
        P(None, WIDE),
        P(None, WIDE),
        P(None, WIDE),
        P(None, WIDE),
    )
    devices = mesh.devices
    lines = Mesh(
        devices.reshape(devices.shape[0], LINE, devices.shape[1] // LINE), ("dp", "line", "spot")
    )
    return jax.shard_map(shards, mesh=lines, in_specs=in_specs, out_specs=out_specs, check_vma=False)
```

```python
import math
from functools import partial

import jax
import jax.numpy as jnp
from jax import lax
from jax.experimental import pallas as pl
from jax.experimental.pallas import tpu as pltpu
from jax.sharding import Mesh
from jax.sharding import PartitionSpec as P

GRID = 24
POOL = 12
SLOTS = 4
STEP = 3
LINE = 4
WIDE = ("line", "spot")
ALL = ("dp", "line", "spot")


beta_one = 0.5
beta_two = 0.5
adam_eps = 1e-08
ema_keep = 0.75
norm_eps = 1e-06


def contract_rows(left, right):
    return lax.dot_general(
        left, right, (((0,), (0,)), ((), ())), preferred_element_type=jnp.float32
    )


def contract_cols(left, right):
    return lax.dot_general(
        left, right, (((1,), (1,)), ((), ())), preferred_element_type=jnp.float32
    )


CHUNK = 48
LANE = 128


def shape_of(shape, kind):
    return jax.ShapeDtypeStruct(shape, kind)


def sigmoid(value):
    return 0.5 * jnp.tanh(0.5 * value) + 0.5


def fold_rows(value):
    return jnp.sum(value.reshape(value.shape[0] // 8, 8, value.shape[1]), axis=0)


def row_span(k, size):
    return pl.ds(pl.multiple_of(k * size, 16), size)


def lane_span(j):
    return pl.ds(j * LANE, LANE)


def row_total(parts):
    total = parts[0]
    for part in parts[1:]:
        total = total + part
    return jnp.sum(total, axis=1, keepdims=True)


def normalize(read, norm_ref, scale_ref, span, finish):
    width = norm_ref.shape[1]
    spans = [lane_span(j) for j in range(width // LANE)]
    center = row_total([read(lanes) for lanes in spans]) * (1.0 / width)
    spread = row_total([jnp.square(read(lanes) - center) for lanes in spans]) * (1.0 / width)
    scale = lax.rsqrt(spread + norm_eps)
    scale_ref[span, :] = jnp.broadcast_to(scale, (span.size, LANE))
    for lanes in spans:
        unit = (read(lanes) - center) * scale
        norm_ref[span, lanes] = unit
        finish(lanes, unit)


def shift_rows(value, amount, mask):
    return pltpu.roll(value, amount % value.shape[0], 0) * mask


def masks_for(side, rows):
    cell = jnp.arange(rows, dtype=jnp.int32)
    x, y = cell % side, (cell // side) % side
    flags = jnp.stack([x > 0, x < side - 1, y > 0, y < side - 1]).astype(jnp.float32)
    return jnp.broadcast_to(flags[:, :, None], (4, rows, LANE))


def conv_block(above, level, below, taps, mask_ref):
    columns = [
        taps[c] * above + taps[3 + c] * level + taps[6 + c] * below for c in range(3)
    ]
    return (
        columns[1]
        + shift_rows(columns[0], 1, mask_ref[0])
        + shift_rows(columns[2], -1, mask_ref[1])
    )


def taps_at(vec_ref, lanes):
    return [vec_ref[k : k + 1, lanes] for k in range(9)]


def forward_kernel(side, *refs):
    pooled = side == GRID
    if pooled:
        x_ref, in_ref, out_ref, vec_ref, mask_ref, pool_ref = refs[:6]
        n1_ref, n2_ref, n3_ref, r1_ref, r2_ref, r3_ref, b_ref, y_ref = refs[6:14]
        lin_ref, act_ref, hi_ref, lo_ref = refs[14:]
    else:
        live_ref, x_ref, in_ref, out_ref, vec_ref, mask_ref = refs[:6]
        n1_ref, n2_ref, n3_ref, r1_ref, r2_ref, r3_ref, b_ref, y_ref = refs[6:14]
        lin_ref, act_ref = refs[14:]
    rows, width = x_ref.shape
    count = rows // CHUNK
    edge = side if pooled else 0
    lin_ref[...] = jnp.dot(x_ref[...], in_ref[...], preferred_element_type=jnp.float32)
    if pooled:
        act_ref[0:side, :] = jnp.zeros((side, width), jnp.float32)
        act_ref[rows + side : rows + 2 * side, :] = jnp.zeros((side, width), jnp.float32)

    @pl.loop(0, count)
    def _(k):
        span = row_span(k, CHUNK)
        above = pl.ds(pl.multiple_of(k * CHUNK + edge, 8), CHUNK)

        def finish(lanes, unit):
            value = unit * vec_ref[9:10, lanes] + vec_ref[10:11, lanes]
            act_ref[above, lanes] = value * sigmoid(value)

        normalize(lambda lanes: lin_ref[span, lanes], n1_ref, r1_ref, span, finish)

    if pooled:

        @pl.loop(0, count)
        def _(k):
            for j in range(width // LANE):
                lanes = lane_span(j)
                near = [
                    act_ref[pl.ds(pl.multiple_of(k * CHUNK + r * side, 8), CHUNK), lanes]
                    for r in range(3)
                ]
                lin_ref[row_span(k, CHUNK), lanes] = conv_block(
                    near[0], near[1], near[2], taps_at(vec_ref, lanes), mask_ref
                )
    else:
        cells = side * side

        @pl.loop(0, rows // cells)
        def _(k):
            for j in range(width // LANE):
                lanes = lane_span(j)
                level = act_ref[row_span(k, cells), lanes]
                lin_ref[row_span(k, cells), lanes] = conv_block(
                    shift_rows(level, side, mask_ref[2]),
                    level,
                    shift_rows(level, -side, mask_ref[3]),
                    taps_at(vec_ref, lanes),
                    mask_ref,
                )

    @pl.loop(0, count)
    def _(k):
        span = row_span(k, CHUNK)

        def finish(lanes, unit):
            value = unit * vec_ref[11:12, lanes] + vec_ref[12:13, lanes]
            b_ref[span, lanes] = (value * sigmoid(value)).astype(jnp.bfloat16)

        normalize(lambda lanes: lin_ref[span, lanes], n2_ref, r2_ref, span, finish)

    lin_ref[...] = jnp.dot(b_ref[...], out_ref[...], preferred_element_type=jnp.float32)

    @pl.loop(0, count)
    def _(k):
        span = row_span(k, CHUNK)
        if not pooled:
            scale = live_ref[k * CHUNK // (side * side)]

        def finish(lanes, unit):
            value = (
                x_ref[span, lanes].astype(jnp.float32)
                + unit * vec_ref[13:14, lanes]
                + vec_ref[14:15, lanes]
            )
            value = value * sigmoid(value)
            if pooled:
                high = value.astype(jnp.bfloat16)
                hi_ref[span, lanes] = high
                lo_ref[span, lanes] = (value - high.astype(jnp.float32)).astype(jnp.bfloat16)
            else:
                y_ref[span, lanes] = (value * scale).astype(jnp.bfloat16)

        normalize(lambda lanes: lin_ref[span, lanes], n3_ref, r3_ref, span, finish)

    if pooled:
        y_ref[...] = (
            jnp.dot(pool_ref[...], hi_ref[...], preferred_element_type=jnp.float32)
            + jnp.dot(pool_ref[...], lo_ref[...], preferred_element_type=jnp.float32)
        ).astype(jnp.bfloat16)


def backward_kernel(side, *refs):
    pooled = side == GRID
    if pooled:
        up_ref, d_ref, x_ref, in_ref, out_ref, vec_ref, mask_ref = refs[:7]
    else:
        live_ref, d_ref, x_ref, in_ref, out_ref, vec_ref, mask_ref = refs[:7]
    n1_ref, n2_ref, n3_ref, r1_ref, r2_ref, r3_ref = refs[7:13]
    dx_ref, da_ref, dc_ref, sum_ref = refs[13:17]
    res_ref, mix_ref, act_ref = refs[17:20]
    rows, width = x_ref.shape
    count = rows // CHUNK
    edge = side if pooled else 0
    spans = [lane_span(j) for j in range(width // LANE)]

    @pl.when(pl.program_id(0) == 0)
    def _():
        sum_ref[...] = jnp.zeros(sum_ref.shape, jnp.float32)

    def add_sum(k, lanes, value):
        sum_ref[8 * k : 8 * k + 8, lanes] += fold_rows(value)

    if pooled:
        grads = d_ref[...]
        high = grads.astype(jnp.bfloat16)
        low = (grads - high.astype(jnp.float32)).astype(jnp.bfloat16)
        res_ref[...] = jnp.dot(
            up_ref[...], high, preferred_element_type=jnp.float32
        ) + jnp.dot(up_ref[...], low, preferred_element_type=jnp.float32)

    def norm_back(unit_ref, scale_ref, span, gain, read_grad, store):
        first, second = [], []
        for lanes in spans:
            grad = read_grad(lanes) * vec_ref[gain : gain + 1, lanes]
            first.append(grad)
            second.append(grad * unit_ref[span, lanes])
        mean_grad = row_total(first) * (1.0 / width)
        mean_unit = row_total(second) * (1.0 / width)
        for lanes in spans:
            grad = read_grad(lanes) * vec_ref[gain : gain + 1, lanes]
            store(
                lanes,
                scale_ref[span, :]
                * (grad - mean_grad - unit_ref[span, lanes] * mean_unit),
            )

    @pl.loop(0, count)
    def _(k):
        span = row_span(k, CHUNK)
        if not pooled:
            scale = live_ref[k * CHUNK // (side * side)]
        for lanes in spans:
            unit = n3_ref[span, lanes]
            value = (
                x_ref[span, lanes].astype(jnp.float32)
                + unit * vec_ref[13:14, lanes]
                + vec_ref[14:15, lanes]
            )
            gate = sigmoid(value)
            grad = res_ref[span, lanes] if pooled else d_ref[span, lanes] * scale
            grad = grad * (gate * (1.0 + value * (1.0 - gate)))
            res_ref[span, lanes] = grad
            add_sum(13, lanes, grad * unit)
            add_sum(14, lanes, grad)

        def store(lanes, value):
            dc_ref[span, lanes] = value.astype(jnp.bfloat16)

        norm_back(n3_ref, r3_ref, span, 13, lambda lanes: res_ref[span, lanes], store)

    if pooled:
        mix_ref[0:side, :] = jnp.zeros((side, width), jnp.float32)
        mix_ref[rows + side : rows + 2 * side, :] = jnp.zeros((side, width), jnp.float32)
    mix_ref[edge : rows + edge, :] = contract_cols(dc_ref[...], out_ref[...])

    @pl.loop(0, count)
    def _(k):
        span = row_span(k, CHUNK)
        at = pl.ds(pl.multiple_of(k * CHUNK + edge, 8), CHUNK)
        for lanes in spans:
            unit = n2_ref[span, lanes]
            value = unit * vec_ref[11:12, lanes] + vec_ref[12:13, lanes]
            gate = sigmoid(value)
            grad = mix_ref[at, lanes] * (gate * (1.0 + value * (1.0 - gate)))
            mix_ref[at, lanes] = grad
            add_sum(11, lanes, grad * unit)
            add_sum(12, lanes, grad)

        def store(lanes, value):
            mix_ref[at, lanes] = value

        norm_back(n2_ref, r2_ref, span, 11, lambda lanes: mix_ref[at, lanes], store)

    size = CHUNK if pooled else side * side

    @pl.loop(0, rows // size)
    def _(k):
        span = row_span(k, size)
        for lanes in spans:
            if pooled:
                near = [
                    mix_ref[pl.ds(pl.multiple_of(k * size + (2 - r) * side, 8), size), lanes]
                    for r in range(3)
                ]
            else:
                level = mix_ref[span, lanes]
                near = [
                    shift_rows(level, -side, mask_ref[3]),
                    level,
                    shift_rows(level, side, mask_ref[2]),
                ]
            taps = taps_at(vec_ref, lanes)
            mixed = [
                taps[c] * near[0] + taps[3 + c] * near[1] + taps[6 + c] * near[2]
                for c in range(3)
            ]
            grad = (
                mixed[1]
                + shift_rows(mixed[0], -1, mask_ref[1])
                + shift_rows(mixed[2], 1, mask_ref[0])
            )
            unit = n1_ref[span, lanes]
            value = unit * vec_ref[9:10, lanes] + vec_ref[10:11, lanes]
            gate = sigmoid(value)
            active = value * gate
            sides = [
                shift_rows(active, 1, mask_ref[0]),
                active,
                shift_rows(active, -1, mask_ref[1]),
            ]
            for r in range(3):
                for c in range(3):
                    add_sum(3 * r + c, lanes, sides[c] * near[r])
            grad = grad * (gate * (1.0 + value * (1.0 - gate)))
            act_ref[span, lanes] = grad
            add_sum(9, lanes, grad * unit)
            add_sum(10, lanes, grad)

    @pl.loop(0, count)
    def _(k):
        span = row_span(k, CHUNK)

        def store(lanes, value):
            da_ref[span, lanes] = value.astype(jnp.bfloat16)

        norm_back(n1_ref, r1_ref, span, 9, lambda lanes: act_ref[span, lanes], store)

    step = 256
    for j in range(width // step):
        dx_ref[:, j * step : (j + 1) * step] = (
            res_ref[:, j * step : (j + 1) * step]
            + contract_cols(da_ref[...], in_ref[j * step : (j + 1) * step, :])
        ).astype(dx_ref.dtype)


def pool_matrix():
    cell = jnp.arange(GRID * GRID, dtype=jnp.int32)
    home = (cell // GRID // 2) * POOL + (cell % GRID) // 2
    spot = jnp.arange(POOL * POOL, dtype=jnp.int32)
    return jnp.where(home[None, :] == spot[:, None], 0.25, 0.0).astype(jnp.bfloat16)


def block_specs(side, rows, width):
    whole = lambda shape: pl.BlockSpec(shape, lambda i: (0,) * len(shape))
    part = lambda cells, lanes: pl.BlockSpec((cells, lanes), lambda i: (i, 0))
    size = side * side if side == GRID else rows
    return whole, part, size


def kernel_params(axes=1):
    return pltpu.CompilerParams(
        dimension_semantics=("arbitrary",) * axes, vmem_limit_bytes=60 * 1024 * 1024
    )


def block_forward(rows, w_in, w_out, vecs, side, live=None):
    total, width = rows.shape
    whole, part, size = block_specs(side, total, width)
    pooled = side == GRID
    mask_rows = CHUNK if pooled else side * side
    vecs = jnp.pad(vecs, ((0, 1), (0, 0)))
    masks = masks_for(side, mask_rows)
    norm = shape_of((total, width), jnp.float32)
    scale = shape_of((total, LANE), jnp.float32)
    out_cells = POOL * POOL if pooled else size
    operands = [rows, w_in, w_out, vecs, masks]
    in_specs = [
        part(size, width),
        whole(w_in.shape),
        whole(w_out.shape),
        whole(vecs.shape),
        whole(masks.shape),
    ]
    scratch = [
        pltpu.VMEM((size, width), jnp.float32),
        pltpu.VMEM((size + 2 * side, width) if pooled else (size, width), jnp.float32),
    ]
    if pooled:
        operands.append(pool_matrix())
        in_specs.append(whole((POOL * POOL, GRID * GRID)))
        scratch += [pltpu.VMEM((size, width), jnp.bfloat16)] * 2
    else:
        operands.insert(0, live)
        in_specs.insert(0, pl.BlockSpec(memory_space=pltpu.SMEM))
    outs = pl.pallas_call(
        partial(forward_kernel, side),
        grid=(total // size,),
        in_specs=in_specs,
        out_specs=[part(size, width)] * 3
        + [part(size, LANE)] * 3
        + [part(size, width), part(out_cells, width)],
        out_shape=[norm] * 3
        + [scale] * 3
        + [
            shape_of((total, width), jnp.bfloat16),
            shape_of((total // size * out_cells, width), jnp.bfloat16),
        ],
        scratch_shapes=scratch,
        compiler_params=kernel_params(),
        name="block_forward_" + str(side),
    )(*operands)
    return outs[7], (rows, outs[6], tuple(outs[:6]))


def block_backward(d_result, saved, w_in, w_out, vecs, side, live=None):
    rows, narrow, kept = saved
    total, width = rows.shape
    whole, part, size = block_specs(side, total, width)
    pooled = side == GRID
    mask_rows = CHUNK if pooled else side * side
    vecs = jnp.pad(vecs, ((0, 1), (0, 0)))
    masks = masks_for(side, mask_rows)
    in_cells = POOL * POOL if pooled else size
    if pooled:
        first = pool_matrix().T
        first_spec = whole(first.shape)
    else:
        first = live
        first_spec = pl.BlockSpec(memory_space=pltpu.SMEM)
    low = shape_of((total, width), jnp.bfloat16)
    dx, da, dc, sums = pl.pallas_call(
        partial(backward_kernel, side),
        grid=(total // size,),
        in_specs=[
            first_spec,
            part(in_cells, width),
            part(size, width),
            whole(w_in.shape),
            whole(w_out.shape),
            whole(vecs.shape),
            whole(masks.shape),
        ]
        + [part(size, width)] * 3
        + [part(size, LANE)] * 3,
        out_specs=[part(size, width)] * 3 + [whole((128, width))],
        out_shape=[
            shape_of((total, width), jnp.bfloat16 if pooled else jnp.float32),
            low,
            low,
            shape_of((128, width), jnp.float32),
        ],
        scratch_shapes=[
            pltpu.VMEM((size, width), jnp.float32),
            pltpu.VMEM((size + 2 * side, width) if pooled else (size, width), jnp.float32),
            pltpu.VMEM((size, width), jnp.float32),
        ],
        compiler_params=kernel_params(),
        name="block_backward_" + str(side),
    )(first, d_result, rows, w_in, w_out, vecs, masks, *kept)
    grad_out = contract_rows(narrow, dc)
    grad_in = contract_rows(rows, da)
    grad_vecs = jnp.sum(sums[:120].reshape(15, 8, width), axis=1)
    return dx, grad_in, grad_out, grad_vecs


def adamw(weight, grad, moment, square, average, rate, decay):
    momentum = beta_one * moment + (1.0 - beta_one) * grad
    variance = beta_two * square + (1.0 - beta_two) * grad * grad
    scaled_m = momentum / (1.0 - beta_one**STEP)
    scaled_v = variance / (1.0 - beta_two**STEP)
    updated = weight - rate * (scaled_m / (jnp.sqrt(scaled_v) + adam_eps) + decay * weight)
    smoothed = ema_keep * average + (1.0 - ema_keep) * updated
    return (updated, momentum, variance, smoothed, updated.astype(jnp.bfloat16))


def pad_row(row, width):
    return jnp.pad(row, ((0, 0), (0, width - row.shape[1])))


def ring_order(chips):
    inner = chips // LINE
    cells = [(o, 0) for o in range(LINE)]
    for turn, o in enumerate(reversed(range(LINE))):
        line = list(range(1, inner))
        cells += [(o, i) for i in (line if turn % 2 == 0 else line[::-1])]
    return [o * inner + i for o, i in cells]


def ring_gather(value, inner, group):
    chips = LINE * inner // 2
    ring = ring_order(chips)
    back = sorted(range(chips), key=lambda place: ring[place])
    index = lax.axis_index(WIDE)
    core = index % 2
    place = jnp.asarray(back, jnp.int32)[index // 2]
    turn = 1 - 2 * core
    pairs = []
    for r in range(chips):
        ahead, behind = ring[(r + 1) % chips], ring[(r - 1) % chips]
        pairs += [(ring[r] * 2, ahead * 2), (ring[r] * 2 + 1, behind * 2 + 1)]
    spots = jnp.asarray(ring, jnp.int32)
    held_all = jnp.zeros((chips,) + value.shape, value.dtype)
    for s in range(chips):
        if s:
            value = lax.ppermute(value, WIDE, pairs)
        if s == chips // 2:
            middle = value
        spot = spots[(place - turn * s) % chips]
        held_all = lax.dynamic_update_index_in_dim(held_all, value, spot, 0)
    if group == 2:
        other = lax.ppermute(held_all, "dp", [(0, 1), (1, 0)])
        first = lax.axis_index("dp") == 0
        planes = jnp.stack(
            [jnp.where(first, held_all, other), jnp.where(first, other, held_all)]
        )
    else:
        planes = lax.all_gather(held_all, "dp", axis=0)
    other = lax.ppermute(planes, "spot", [(i, i ^ 1) for i in range(inner)])
    first = core == 0
    planes = jnp.stack([jnp.where(first, planes, other), jnp.where(first, other, planes)], axis=2)
    return planes, middle


def swap_groups(value, group):
    return lax.ppermute(value, "dp", [(i, i ^ 1) for i in range(group)])


def over_groups(value, group):
    if group == 2:
        other = lax.ppermute(value, "dp", [(0, 1), (1, 0)])
        return value.astype(jnp.float32) + other.astype(jnp.float32)
    return lax.psum(value, "dp").astype(jnp.float32)


def reduce_block(grad_in, grad_out, grad_vecs, devices):
    width = grad_in.shape[1]
    share = width // devices
    rows = [
        grad_in.astype(jnp.bfloat16).reshape(devices, share, width),
        grad_out.astype(jnp.bfloat16).reshape(devices, share, width),
        jnp.pad(
            grad_vecs.astype(jnp.bfloat16)
            .reshape(15, devices, share)
            .transpose(1, 0, 2)
            .reshape(devices, 1, 15 * share),
            ((0, 0), (0, 15), (0, width - 15 * share)),
        ),
    ]
    return jnp.concatenate(rows, axis=1)


def pick(value, at, axis):
    return lax.dynamic_index_in_dim(value, at, axis, False)


def after(value, *others):
    return lax.optimization_barrier((value,) + others)[0]


def spread_reduce(blocks, works):
    count = blocks.shape[0]
    bits = count.bit_length() - 1
    order = [0, 1] + list(range(bits - 1, 1, -1))
    me = lax.axis_index(ALL)
    blocks = blocks.reshape((2,) * bits + blocks.shape[1:])
    left = list(range(bits))[::-1]
    for stage, bit in enumerate(order):
        axis = left.index(bit)
        left.pop(axis)
        mine = (me >> bit) & 1
        pairs = [(i, i ^ (1 << bit)) for i in range(count)]
        sent = pick(blocks, 1 - mine, axis)
        theirs = lax.ppermute(sent, ALL, pairs)
        if stage < len(works):
            theirs = after(theirs, works[stage](blocks))
        blocks = (
            pick(blocks, mine, axis).astype(jnp.float32) + theirs.astype(jnp.float32)
        ).astype(jnp.bfloat16)
    return blocks


def held(value):
    return lax.optimization_barrier(value)


def gelu_slope(value):
    return 0.5 * (1.0 + lax.erf(value * (0.5**0.5))) + value * jnp.exp(-0.5 * value * value) * (
        0.5 / math.pi
    ) ** 0.5


def hidden_kernel(tokens_ref, expand_ref, bias_ref, out_ref):
    pre = jnp.dot(tokens_ref[...], expand_ref[...], preferred_element_type=jnp.float32)
    pre = pre + bias_ref[...]
    out_ref[...] = (0.5 * pre * (1.0 + lax.erf(pre * (0.5**0.5)))).astype(jnp.bfloat16)


def hidden_forward(tokens, readers, bias, half):
    total, width = tokens.shape
    depth = readers.shape[1] // 2
    rows, step = total // LINE, 512
    skip = half * depth // step
    return pl.pallas_call(
        hidden_kernel,
        grid=(depth // step, LINE),
        in_specs=[
            pl.BlockSpec((rows, width), lambda j, i: (i, 0)),
            pl.BlockSpec((width, step), lambda j, i: (0, j + skip)),
            pl.BlockSpec((1, step), lambda j, i: (0, j + skip)),
        ],
        out_specs=pl.BlockSpec((rows, step), lambda j, i: (i, j)),
        out_shape=shape_of((total, depth), jnp.bfloat16),
        compiler_params=kernel_params(2),
        name="hidden_forward",
    )(tokens, readers, bias[None])


def adamw_kernel(rate, decay, grad_ref, *refs):
    old, new = refs[:4], refs[4:]
    results = adamw(old[0][...], grad_ref[...].T, *[ref[...] for ref in old[1:]], rate, decay)
    for ref, result in zip(new, results):
        ref[...] = result


def adamw_turned(weight, grad, moment, square, average, rate, decay):
    depth, columns = weight.shape
    step = 512
    part = pl.BlockSpec((step, columns), lambda i: (i, 0))
    return pl.pallas_call(
        partial(adamw_kernel, rate, decay),
        grid=(depth // step,),
        in_specs=[pl.BlockSpec((columns, step), lambda i: (0, i))] + [part] * 4,
        out_specs=[part] * 5,
        out_shape=[shape_of(weight.shape, jnp.float32)] * 4
        + [shape_of(weight.shape, jnp.bfloat16)],
        compiler_params=kernel_params(),
        name="adamw_turned",
    )(grad, weight, moment, square, average)


def pre_kernel(counts, at_ref, d_ref, tokens_ref, *refs):
    sources, (expand_ref, bias_ref, out_ref) = refs[: len(counts)], refs[len(counts) :]
    pre = jnp.dot(tokens_ref[...], expand_ref[...], preferred_element_type=jnp.float32)
    slope = gelu_slope(pre + bias_ref[...])
    index = pl.program_id(0)
    start = 0
    for count, source in zip(counts, sources):

        @pl.when((index >= start) & (index < start + count))
        def _(source=source):
            grad = contract_cols(d_ref[...], source[...])
            out_ref[...] = (grad * slope).astype(jnp.bfloat16)

        start += count


def pre_backward(d_full, tokens, shared, bias, pieces):
    rows, width = tokens.shape
    depth = d_full.shape[1]
    step = 512
    counts = [size // step for _, _, _, size in pieces]
    order = jnp.concatenate(
        [
            jnp.asarray(start // step, jnp.int32) + jnp.arange(size // step, dtype=jnp.int32)
            for _, _, start, size in pieces
        ]
    )
    specs = []
    first = 0
    for (source, skip, _, size), count in zip(pieces, counts):
        low, high = skip // step, skip // step + count - 1
        specs.append(
            pl.BlockSpec(
                (step, depth),
                lambda i, at, low=low, high=high, first=first: (
                    jnp.clip(i - first + low, low, high),
                    0,
                ),
            )
        )
        first += count
    return pl.pallas_call(
        partial(pre_kernel, counts),
        grid_spec=pltpu.PrefetchScalarGridSpec(
            num_scalar_prefetch=1,
            grid=(depth // step,),
            in_specs=[
                pl.BlockSpec((rows, depth), lambda i, at: (0, 0)),
                pl.BlockSpec((rows, width), lambda i, at: (0, 0)),
            ]
            + specs
            + [
                pl.BlockSpec((width, step), lambda i, at: (0, at[i])),
                pl.BlockSpec((1, step), lambda i, at: (0, at[i])),
            ],
            out_specs=pl.BlockSpec((rows, step), lambda i, at: (0, at[i])),
        ),
        out_shape=shape_of((rows, depth), jnp.bfloat16),
        compiler_params=kernel_params(),
        name="pre_backward",
    )(order, d_full, tokens, *[piece[0] for piece in pieces], shared, bias[None])


def shards(
    patches,
    counts,
    cotangent,
    filters,
    filters_moment,
    filters_square,
    filters_average,
    vectors,
    vectors_moment,
    vectors_square,
    vectors_average,
    expand,
    expand_moment,
    expand_square,
    expand_average,
    project,
    project_moment,
    project_square,
    project_average,
    offsets,
    offsets_moment,
    offsets_square,
    offsets_average,
):
    inner = lax.axis_size("spot")
    wide = LINE * inner
    group = lax.axis_size("dp")
    devices = wide * group
    share = filters.shape[1]
    lanes = vectors.shape[2]
    columns = expand.shape[1]
    packed = jnp.concatenate(
        [
            filters.astype(jnp.bfloat16).reshape(4 * share, filters.shape[2]),
            pad_row(vectors.astype(jnp.bfloat16).reshape(1, -1), filters.shape[2]),
            pad_row(offsets.astype(jnp.bfloat16).reshape(1, -1), filters.shape[2]),
            jnp.zeros((14, filters.shape[2]), jnp.bfloat16),
        ]
    )
    spread, middle = ring_gather(packed, inner, group)
    whole_filters = [
        spread[:, :, :, k * share : (k + 1) * share].reshape(devices * share, -1)
        for k in range(4)
    ]
    spread = spread[:, :, :, 4 * share : 4 * share + 2].reshape(devices, 2, -1)
    vec_full = (
        spread[:, 0, : 30 * lanes]
        .reshape(devices, 2, 15, lanes)
        .transpose(1, 2, 0, 3)
        .reshape(2, 15, devices * lanes)
        .astype(jnp.float32)
    )
    full_offsets = (
        spread[:wide, 1, : 2 * columns]
        .reshape(wide, 2, columns)
        .transpose(1, 0, 2)
        .reshape(2, wide * columns)
        .astype(jnp.float32)
    )
    images = patches.shape[0]
    width = patches.shape[2]
    samples = counts.shape[0]
    image_index = jnp.arange(images, dtype=jnp.int32)
    owner = image_index // SLOTS
    slot = image_index % SLOTS
    matches = owner[:, None] == jnp.arange(samples, dtype=jnp.int32)[None, :]
    chosen = jnp.sum(jnp.where(matches, counts[None, :], 0), axis=1)
    live = (slot < chosen).astype(jnp.float32)
    rows = patches.reshape(images * GRID * GRID, width)
    d_cols = cotangent.reshape(-1, columns)
    part = d_cols.shape[0] // wide
    plane = lax.axis_index("dp") % 2
    swap = [(i, i ^ 1) for i in range(inner)]
    cross = [(i, i ^ 1) for i in range(group)]
    core = lax.axis_index("spot") % 2
    depth = project.shape[0]
    quarter = depth // 4
    project_low = project.astype(jnp.bfloat16)
    own = lax.dynamic_slice_in_dim(project_low, depth // 2 + plane * quarter, quarter, 0)
    shared = jnp.concatenate([expand.astype(jnp.bfloat16), project_low[: depth // 2]])
    own = lax.all_gather(own, WIDE, axis=1, tiled=True)
    shared = lax.all_gather(after(shared, middle), WIDE, axis=1, tiled=True)
    near = pick(after(own, whole_filters[0]).reshape(2, quarter // 2, -1), core, 0)
    near = lax.ppermute(near, "dp", cross)
    pooled, first_saved = block_forward(
        rows, whole_filters[0], whole_filters[1], vec_full[0], GRID
    )
    tokens, second_saved = block_forward(
        pooled, whole_filters[2], whole_filters[3], vec_full[1], POOL, live
    )
    near = after(near, tokens)
    far = lax.ppermute(near, "spot", swap)
    d_full = lax.all_to_all(d_cols, WIDE, split_axis=0, concat_axis=0, tiled=True)
    d_full = after(d_full, whole_filters[0]).reshape(wide, part, columns)
    d_full = d_full.transpose(1, 0, 2).reshape(part, wide * columns)
    g_out = jnp.sum(d_cols.astype(jnp.float32), axis=0)
    d_line = d_cols.reshape(LINE, inner, part, columns).transpose(1, 0, 2, 3)
    tokens_after, shared, d_line, d_full, g_out = lax.optimization_barrier(
        (tokens, shared, d_line, d_full, g_out)
    )
    full_expand = shared[:width]
    tokens_line = lax.all_gather(tokens_after, "line", axis=0, tiled=True)
    d_line = lax.all_to_all(d_line, "spot", split_axis=0, concat_axis=0, tiled=True)
    d_line = d_line.reshape(inner, LINE * part, columns)
    d_cores = d_line.reshape(inner // 2, 2, LINE * part, columns)
    near_at = depth // 2 + (1 - plane) * quarter + core * (quarter // 2)
    far_at = depth // 2 + (1 - plane) * quarter + (1 - core) * (quarter // 2)
    d_pre = pre_backward(
        d_full,
        tokens,
        shared,
        full_offsets[0],
        [
            (shared, width, 0, depth // 2),
            (own, 0, depth // 2 + plane * quarter, quarter),
            (near, 0, near_at, quarter // 2),
            (far, 0, far_at, quarter // 2),
        ],
    )
    d_tokens = contract_cols(d_pre, full_expand)
    d_pooled, g_in_two, g_out_two, g_vec_two = block_backward(
        d_tokens, second_saved, whole_filters[2], whole_filters[3], vec_full[1], POOL, live
    )
    g_two = reduce_block(g_in_two, g_out_two, g_vec_two, devices)
    d_pooled, g_two, d_theirs, d_mine = held(
        (d_pooled, g_two, pick(d_cores, 1 - core, 1), pick(d_cores, core, 1))
    )
    g_two = lax.psum_scatter(g_two, ALL, scatter_dimension=0, tiled=False)
    d_rows, g_in_one, g_out_one, g_vec_one = block_backward(
        d_pooled, first_saved, whole_filters[0], whole_filters[1], vec_full[0], GRID
    )
    patch_gradient = d_rows.reshape(images, GRID * GRID, width)
    g_one = reduce_block(g_in_one, g_out_one, g_vec_one, devices)
    got = {}

    def expand_work(done):
        ones = jnp.ones((tokens.shape[0], 1), jnp.bfloat16)
        more = [after(tokens, done), ones, jnp.zeros((tokens.shape[0], 15), jnp.bfloat16)]
        got["expand"] = contract_rows(jnp.concatenate(more, axis=1), d_pre).astype(jnp.bfloat16)
        return got["expand"]

    def hidden_work(half, done):
        tokens_all = after(tokens_line, done)
        got["hidden", half] = hidden_forward(tokens_all, shared, full_offsets[0], half)
        return got["hidden", half]

    def project_part(d_part, half):
        return lax.dot_general(
            d_part,
            got["hidden", half],
            (((1,), (0,)), ((), ())),
            preferred_element_type=jnp.float32,
        )

    def theirs_work(half, *done):
        theirs = project_part(after(d_theirs, *done), half).astype(jnp.bfloat16)
        got["sent", half] = lax.ppermute(theirs, "spot", [(i, i ^ 1) for i in range(inner)])
        return theirs

    def mine_work(half, done):
        d_part = after(d_mine, done)
        if half == 0:
            d_part, got["two"] = held((d_part, g_two))
        mine = project_part(d_part, half)
        got["sum", half] = mine + got["sent", half].astype(jnp.float32)
        spot = lax.axis_index("spot") // 2
        halves = got["sum", half].reshape(inner // 4, 2, columns, -1)
        theirs = pick(halves, 1 - spot % 2, 1).astype(jnp.bfloat16)
        got["sent", half] = lax.ppermute(theirs, "spot", [(i, i ^ 2) for i in range(inner)])
        return theirs

    def finish_work(half, done):
        spot = lax.axis_index("spot") // 2
        total = got["sum", half].reshape(inner // 4, 2, columns, -1)
        theirs = after(got["sent", half], done)
        total = pick(total, spot % 2, 1) + theirs.astype(jnp.float32)
        step = 4
        while total.shape[0] > 1:
            spot = spot // 2
            halves = total.reshape(total.shape[0] // 2, 2, columns, -1)
            theirs = pick(halves, 1 - spot % 2, 1).astype(jnp.bfloat16)
            theirs = lax.ppermute(theirs, "spot", [(i, i ^ step) for i in range(inner)])
            total = pick(halves, spot % 2, 1) + theirs.astype(jnp.float32)
            step *= 2
        total = total[0].astype(jnp.bfloat16)
        got["total", half] = total
        got["sent", half] = swap_groups(total, group)
        return total

    def swap_work(half, done):
        total = got["total", half]
        other = after(got["sent", half], done)
        got["project", half] = total.astype(jnp.float32) + other.astype(jnp.float32)
        if group != 2:
            got["project", half] = over_groups(total, group)
        return got["project", half]

    def work_two(done):
        return hidden_work(0, done)

    def work_three(done):
        sent = mine_work(0, theirs_work(0, done))
        got["order"] = finish_work(0, hidden_work(1, sent))
        return got["order"]

    def work_four(done):
        return mine_work(1, theirs_work(1, done, got["order"]))

    at = lax.axis_index("line") * inner * columns
    other = jnp.concatenate(
        [
            lax.dynamic_slice_in_dim(piece, at, inner * columns, 1)
            for piece in (near, far)
        ]
    )
    other = jnp.roll(other.reshape(2, quarter // 2, -1), core, 0).reshape(quarter, -1)
    sides = jnp.stack([lax.dynamic_slice_in_dim(own, at, inner * columns, 1), other])
    column_sides = jnp.roll(sides, plane, 0).reshape(2 * quarter, -1)
    column_shared = lax.dynamic_slice(
        shared, (width, at), (depth // 2, inner * columns)
    )
    got["columns", 0] = column_shared
    got["columns", 1] = column_sides

    def readout_part(half, *done):
        return jnp.dot(
            after(got["hidden", half], *done),
            got["columns", half],
            preferred_element_type=jnp.float32,
        )

    def work_five(done):
        at = lax.axis_index("line") * inner * columns
        bias = lax.dynamic_slice_in_dim(full_offsets[1], at, inner * columns, 0)
        out = readout_part(0, done) + bias
        first = swap_work(0, out)
        out = out + readout_part(1, first)
        finish_work(1, out)
        got["out"] = out.astype(jnp.bfloat16)
        return got["out"]

    def work_last(done):
        return work_five(work_four(done))

    g_one = spread_reduce(g_one, [expand_work, work_two, work_three, work_last])
    swap_work(1, got["out"])
    g_expand = lax.psum_scatter(got["expand"], WIDE, scatter_dimension=1, tiled=True)
    out_line = held(
        got["out"].reshape(LINE * part, inner, columns).transpose(1, 0, 2)
    )
    g_expand = after(g_expand, out_line)
    g_expand = jnp.concatenate(
        [g_expand[: width + 1], g_out[None].astype(jnp.bfloat16), g_expand[width + 2 :]]
    )
    g_expand = over_groups(g_expand, group)
    g_offsets = g_expand[width : width + 2]
    g_expand = g_expand[:width]
    g_project = jnp.concatenate([got["project", 0], got["project", 1]], axis=1)
    out_cols = lax.all_to_all(out_line, "spot", split_axis=0, concat_axis=0, tiled=True)
    readout = (
        out_cols.reshape(inner, LINE, part, columns)
        .transpose(1, 0, 2, 3)
        .reshape(-1, POOL * POOL, columns)
    )
    g_two = got["two"]
    g_filters = jnp.stack(
        [g_one[:share], g_one[share : 2 * share], g_two[:share], g_two[share : 2 * share]]
    ).astype(jnp.float32)
    g_vectors = jnp.stack(
        [g_one[2 * share, : 15 * lanes], g_two[2 * share, : 15 * lanes]]
    ).reshape(2, 15, lanes).astype(jnp.float32)
    filters_out = adamw(
        filters, g_filters, filters_moment, filters_square, filters_average, 0.03, 0.05
    )
    vectors_out = adamw(
        vectors, g_vectors, vectors_moment, vectors_square, vectors_average, 0.3, 0.0
    )
    expand_out = adamw(expand, g_expand, expand_moment, expand_square, expand_average, 0.03, 0.05)
    project_out = adamw_turned(
        project, g_project, project_moment, project_square, project_average, 0.016, 0.05
    )
    offsets_out = adamw(
        offsets, g_offsets, offsets_moment, offsets_square, offsets_average, 0.1, 0.0
    )
    return (
        readout,
        patch_gradient,
        filters_out[0],
        filters_out[1],
        filters_out[2],
        filters_out[3],
        filters_out[4],
        vectors_out[0],
        vectors_out[1],
        vectors_out[2],
        vectors_out[3],
        vectors_out[4],
        expand_out[0],
        expand_out[1],
        expand_out[2],
        expand_out[3],
        expand_out[4],
        project_out[0],
        project_out[1],
        project_out[2],
        project_out[3],
        project_out[4],
        offsets_out[0],
        offsets_out[1],
        offsets_out[2],
        offsets_out[3],
        offsets_out[4],
    )


def solution(mesh):
    in_specs = (
        P(ALL, None, None),
        P(ALL),
        P("dp", None, WIDE),
        P(None, ALL, None),
        P(None, ALL, None),
        P(None, ALL, None),
        P(None, ALL, None),
        P(None, None, ALL),
        P(None, None, ALL),
        P(None, None, ALL),
        P(None, None, ALL),
        P(None, WIDE),
        P(None, WIDE),
        P(None, WIDE),
        P(None, WIDE),
        P(None, WIDE),
        P(None, WIDE),
        P(None, WIDE),
        P(None, WIDE),
        P(None, WIDE),
        P(None, WIDE),
        P(None, WIDE),
        P(None, WIDE),
    )
    out_specs = (
        P("dp", None, WIDE),
        P(ALL, None, None),
        P(None, ALL, None),
        P(None, ALL, None),
        P(None, ALL, None),
        P(None, ALL, None),
        P(None, ALL, None),
        P(None, None, ALL),
        P(None, None, ALL),
        P(None, None, ALL),
        P(None, None, ALL),
        P(None, None, ALL),
        P(None, WIDE),
        P(None, WIDE),
        P(None, WIDE),
        P(None, WIDE),
        P(None, WIDE),
        P(None, WIDE),
        P(None, WIDE),
        P(None, WIDE),
        P(None, WIDE),
        P(None, WIDE),
        P(None, WIDE),
        P(None, WIDE),
        P(None, WIDE),
        P(None, WIDE),
        P(None, WIDE),
    )
    devices = mesh.devices
    lines = Mesh(
        devices.reshape(devices.shape[0], LINE, devices.shape[1] // LINE), ("dp", "line", "spot")
    )
    return jax.shard_map(shards, mesh=lines, in_specs=in_specs, out_specs=out_specs, check_vma=False)
```
